256 devices in a mesh: blk: 64 (over y, z, x_lo), inner: 4 (over x_hi, core).
Axes of the slice: x: 4 (x_hi: 2, x_lo: 2; x = x_hi * 2 + x_lo), y: 4, z: 8, core: 2. Of those that a mesh axis runs over, the one named last changes fastest.
Arguments:
- density: float32 [512, 9, 128, 128], P(('blk', 'inner')), may hold values from -0.5 to 0.5
- block_cols: int32 [512, 9], P(('blk', 'inner')), may hold values from 0 to 511, as said below
- targets: int32 [512, 9, 9], P(('blk', 'inner')), may hold values from 0 to 9, as said below
Outputs:
- purified: float32 [512, 9, 128, 128], P(('blk', 'inner'))
The draws below stay inside these ranges and needn't reach their ends.
Inputs may be any that keep to these rules, and one draw needn't show every extreme that they name: `block_cols`: strips are runs of 8 block rows. Slots 0 .. 2, 3 .. 5 and 6 .. 8 of row k hold 3 distinct columns each, ascending, from the strip before k's own (cyclically), k's own strip, and the strip after it (cyclically); the own group always contains column k. targets[k, s, t] is the slot u with block_cols[block_cols[k, s], u] == block_cols[k, t], or 9 where row block_cols[k, s] does not store that column.
All inputs are finite; a program needn't handle non-finite values.
Results may differ from the reference program's by a relative error of at most 0.0001.
Values sent between devices are 32-bit elements; how exact they have to be, the bound alone decides.
A program may use at most 128 MiB of HBM per device.

```python
import jax
import jax.numpy as jnp
from jax import lax

B = 128
STRIP = 8
PER = 3
NZ = 9
NB = 512


def pattern(key):
    base_key = jax.random.fold_in(key, 7)
    strips = NB // STRIP
    row_ids = jnp.arange(NB, dtype=jnp.int32)
    home_strip = row_ids // STRIP
    own_slot = row_ids % STRIP
    scores = jax.random.randint(base_key, (NB, 3, STRIP), 0, 1 << 20)
    unique_entries = scores * STRIP + jnp.arange(STRIP, dtype=jnp.int32)[None, None, :]
    forced = (jnp.arange(3)[None, :, None] == 1) & (jnp.arange(STRIP)[None, None, :] == own_slot[:, None, None])
    unique_entries = jnp.where(forced, -1, unique_entries)
    ranked = jnp.argsort(unique_entries, axis=-1)[:, :, :PER]
    chosen = jnp.sort(ranked, axis=-1).astype(jnp.int32)
    strip_of = (home_strip[:, None] + jnp.arange(-1, 2, dtype=jnp.int32)[None, :]) % strips
    block_cols = (strip_of[:, :, None] * STRIP + chosen).reshape(NB, NZ).astype(jnp.int32)
    neighbour_cols = block_cols[block_cols]
    matches = neighbour_cols[:, :, None, :] == block_cols[:, None, :, None]
    present = jnp.any(matches, axis=-1)
    slot_index = jnp.sum(jnp.where(matches, jnp.arange(NZ, dtype=jnp.int32), 0), axis=-1)
    targets = jnp.where(present, slot_index, NZ).astype(jnp.int32)
    return (block_cols, targets)


def draw_block_cols(key, part):
    return pattern(key)[0]


def draw_targets(key, part):
    return pattern(key)[1]


def block_levels(own_key, dims, cuts, smallest, largest):
    level, own = 1.0, jax.random.fold_in(own_key, 6)
    for position, blocks in cuts:
        heights = jnp.exp(jax.random.uniform(jax.random.fold_in(own, position), (blocks,), jnp.float32, smallest / len(cuts), largest / len(cuts)))
        level = level * jnp.repeat(heights, dims[position] // blocks).reshape([-1 if axis == position else 1 for axis in range(len(dims))])
    return level


def bell_draw(stream_key, shape, deviation, most, shards=(), held_as=jnp.bfloat16):
    entries = deviation * jax.random.normal(stream_key, shape, jnp.float32)
    if shards:
        entries = entries * block_levels(stream_key, shape, shards, -0.22, 0.18)
    return jnp.clip(entries, -most, most).astype(held_as)


def setup_inputs(seed: int = 0) -> dict:
    keys = jax.random.split(jax.random.key(seed), 4)
    return {
        "density": bell_draw(keys[0], (NB, NZ, B, B), 0.08, 0.5, ((0, 256),), jnp.float32),
        "block_cols": draw_block_cols(jax.random.fold_in(keys[3], 71), 0),
        "targets": draw_targets(jax.random.fold_in(keys[3], 71), 0),
    }


def reference(density, block_cols, targets):
    row_total, slot_total, block_side, _ = density.shape

    def accumulate_row(row_position_index, square):
        matrix_blocks = density[row_position_index]
        block_products = jnp.einsum("rzd,wzg->rwdg", matrix_blocks, matrix_blocks, precision=lax.Precision.HIGHEST)
        destination_rows = jnp.broadcast_to(block_cols[row_position_index][:, None], (slot_total, slot_total))
        dest_slots = targets[row_position_index]
        return square.at[destination_rows, dest_slots].add(block_products, mode="drop")

    square = lax.fori_loop(0, row_total, accumulate_row, jnp.zeros_like(density))
    return 2.0 * density - square
```

```python
import functools

import jax
import jax.numpy as jnp
from jax import lax
from jax.experimental import pallas as pl
from jax.experimental.pallas import tpu as pltpu
from jax.sharding import PartitionSpec as P

MESH = pl.DeviceIdType.MESH
PER = 3
NZ = 9
HALF = 6
X = 4
ROWS = 2


def gather_kernel(
    den, cols, own1, far, side, zrow, table,
    side_s, side_r, far_s, far_r, z_s, z_r,
    mown_s, mown_r, mfar_s, mfar_r, mside_s, mside_r, mz_s, mz_r,
    cols_s, cols_r, local_s,
):
    blk = lax.axis_index("blk")
    inner = lax.axis_index("inner")
    strips = lax.axis_size("blk")
    parity = lax.rem(blk, 2)
    core = lax.rem(inner, 2)
    chip_x = 2 * (inner // 2) + parity

    def at_x(x):
        x = lax.rem(x, X)
        return (blk - parity + lax.rem(x, 2), 2 * (x // 2) + core)

    right, left = at_x(chip_x + 1), at_x(chip_x + X - 1)
    mirror = (blk, inner + 1 - 2 * core)
    z_to = (lax.rem(blk + strips + 2 - 4 * parity, strips), inner)
    z_from = (lax.rem(blk + strips - 2 + 4 * parity, strips), inner)

    def peer(offset, other):
        return (lax.rem(blk + offset + strips, strips), lax.rem(inner + other, 4))

    peers = [(o, i) for o in (-1, 0, 1) for i in range(4) if (o, i) != (0, 0)]
    barrier = pltpu.get_barrier_semaphore()
    for o, i in peers:
        pl.semaphore_signal(barrier, inc=1, device_id=peer(o, i), device_id_type=MESH)
    for device in (z_to, z_from):
        pl.semaphore_signal(barrier, inc=1, device_id=device, device_id_type=MESH)
    pl.semaphore_wait(barrier, len(peers) + 2)

    sent = []

    def send(src, dst, s, r, device):
        copy = pltpu.make_async_remote_copy(
            src_ref=src, dst_ref=dst, send_sem=s, recv_sem=r,
            device_id=device, device_id_type=MESH,
        )
        copy.start()
        sent.append(copy)

    def arrived(dst, r):
        pltpu.make_async_remote_copy(
            src_ref=dst, dst_ref=dst, send_sem=r, recv_sem=r,
            device_id=mirror, device_id_type=MESH,
        ).wait_recv()

    def groups(p):
        return (1, 2 * p, 2 - 2 * p)

    def slots(group):
        return pl.ds(PER * group, PER)

    mine = groups(parity)
    theirs = groups(1 - parity)
    z_place = (PER * parity, PER * (1 - parity))

    for n in range(6):
        g, row = n // 2, n % 2
        cut = slots(mine[g])
        for sd, device in ((0, right), (1, left)):
            send(den.at[row, cut], side.at[0, sd, row, cut],
                 side_s.at[sd, n], side_r.at[sd, n], device)
    for k, (o, i) in enumerate(peers):
        send(cols, table.at[1 - o, inner], cols_s.at[k], cols_r.at[1 - o, inner], peer(o, i))
    local = pltpu.make_async_copy(cols, table.at[1, inner], local_s)
    local.start()
    for n in range(6):
        g, row = n // 2, n % 2
        cut = slots(g)
        send(den.at[row, cut], own1.at[row, cut], mown_s.at[n], mown_r.at[n], mirror)

    def z_arrived(m):
        g, row, sd = m // 4, (m // 2) % 2, m % 2
        place = pl.ds(z_place[g], PER)
        arrived(zrow.at[0, sd, row, place], z_r.at[m])
        send(zrow.at[0, sd, row, place], zrow.at[1, sd, row, place],
             mz_s.at[m], mz_r.at[m], mirror)

    def far_arrived(j):
        for row in range(2):
            cut = slots(mine[j])
            arrived(far.at[0, row, cut], far_r.at[row, j])
            send(far.at[0, row, cut], far.at[1, row, cut],
                 mfar_s.at[row, j], mfar_r.at[row, j], mirror)

    for n in range(6):
        g, row = n // 2, n % 2
        cut = slots(theirs[g])
        for sd in range(2):
            arrived(side.at[0, sd, row, cut], side_r.at[sd, n])
            if g < 2:
                m = 2 * n + sd
                send(side.at[0, sd, row, cut],
                     zrow.at[0, sd, row, pl.ds(z_place[g], PER)],
                     z_s.at[m], z_r.at[m], z_to)
            if row == sd:
                send(side.at[0, sd, row, cut], far.at[0, row, cut],
                     far_s.at[row, g], far_r.at[row, g], (right, left)[sd])
            if g != 1:
                m = 2 * row + sd + (4 if g == 2 else 0)
                send(side.at[0, sd, row, cut], side.at[1, sd, row, cut],
                     mside_s.at[m], mside_r.at[m], mirror)
        if n >= 2:
            z_arrived(n - 2)
    far_arrived(0)
    z_arrived(4)
    z_arrived(5)
    far_arrived(1)
    z_arrived(6)
    z_arrived(7)
    far_arrived(2)

    for n in range(6):
        g, row = n // 2, n % 2
        arrived(own1.at[row, slots(g)], mown_r.at[n])
        arrived(far.at[1, row, slots(mine[g])], mfar_r.at[row, g])
        for sd in range(2):
            if g != 1:
                m = 2 * row + sd + (4 if g == 2 else 0)
                arrived(side.at[1, sd, row, slots(theirs[g])], mside_r.at[m])
            if g < 2:
                m = 2 * n + sd
                arrived(zrow.at[1, sd, row, pl.ds(z_place[g], PER)], mz_r.at[m])
    local.wait()
    for o, i in peers:
        other = lax.rem(inner + i, 4)
        arrived(table.at[1 + o, other], cols_r.at[1 + o, other])
    for copy in sent:
        copy.wait_send()


def gather(density, block_cols):
    rows, nz, b, _ = density.shape
    f32 = density.dtype
    dma = pltpu.SemaphoreType.DMA
    anywhere = pl.BlockSpec(memory_space=pl.ANY)
    return pl.pallas_call(
        gather_kernel,
        out_shape=(
            jax.ShapeDtypeStruct((rows, nz, b, b), f32),
            jax.ShapeDtypeStruct((2, rows, nz, b, b), f32),
            jax.ShapeDtypeStruct((2, 2, rows, nz, b, b), f32),
            jax.ShapeDtypeStruct((2, 2, rows, HALF, b, b), f32),
            jax.ShapeDtypeStruct((3, 4, rows, nz), jnp.int32),
        ),
        in_specs=[anywhere, anywhere],
        out_specs=(anywhere,) * 5,
        scratch_shapes=[
            dma((2, 6)), dma((2, 6)), dma((2, 3)), dma((2, 3)), dma((8,)), dma((8,)),
            dma((6,)), dma((6,)), dma((2, 3)), dma((2, 3)),
            dma((8,)), dma((8,)), dma((8,)), dma((8,)),
            dma((11,)), dma((3, 4)), dma,
        ],
        compiler_params=pltpu.CompilerParams(collective_id=0, has_side_effects=True),
    )(density, block_cols)


def product_kernel(
    where, table, den, own1, far, side, zrow, out,
    held, acc, sem,
):
    blk, inner = where[0], where[1]
    parity = lax.rem(blk, 2)
    chip_x = 2 * (inner // 2) + parity
    core = lax.rem(inner, 2)
    side_low = PER * parity
    z_low = PER * (1 - parity)

    def source(q):
        if q < 2:
            return den.at[q], held.at[q]
        if q < 4:
            return own1.at[q - 2], held.at[q]
        if q < 8:
            return far.at[(q - 4) // 2, q % 2], held.at[q]
        if q < 16:
            m = q - 8
            cut = pl.ds(side_low, HALF)
            return side.at[m // 4, (m // 2) % 2, m % 2, cut], held.at[q, cut]
        m = q - 16
        return zrow.at[m // 4, (m // 2) % 2, m % 2], held.at[q, pl.ds(z_low, HALF)]

    copies = [pltpu.make_async_copy(*source(q), sem.at[q]) for q in range(24)]
    for copy in copies:
        copy.start()
    acc[...] = jnp.zeros_like(acc)

    def split(value):
        high = value.astype(jnp.bfloat16)
        return high, (value - high.astype(jnp.float32)).astype(jnp.bfloat16)

    def row_products(q, offset, owner, row, first, count):
        group = 2 - offset
        for mine in range(ROWS):
            me = blk * (4 * ROWS) + inner * ROWS + mine
            slot = jnp.int32(-1)
            for a in range(PER):
                s = PER * group + a
                slot = jnp.where(table[offset, owner, row, s] == me, s, slot)

            @pl.when(slot >= 0)
            def _():
                left = held[q, slot].T
                left_high, left_low = split(left)
                lhs = jnp.concatenate([left_high, left_low, left_high], axis=1)
                for t in range(count):
                    right_high, right_low = split(held[q, first + t])
                    rhs = jnp.concatenate([right_high, right_high, right_low], axis=0)
                    product = jnp.dot(lhs, rhs, preferred_element_type=jnp.float32)
                    e = offset - 1 + (first + t) // PER
                    column = table[offset, owner, row, first + t]
                    place = jnp.int32(NZ)
                    for a in range(PER):
                        u = PER * e + a
                        place = jnp.where(table[1, inner, mine, u] == column, u, place)
                    acc[mine, place] += product

    for q in range(24):
        copies[q].wait()
        row = q % 2
        if q < 8:
            owner = (inner, inner + 1 - 2 * core, lax.rem(inner + 2, 4),
                     lax.rem(inner + 2, 4) + 1 - 2 * core)[q // 2]
            row_products(q, 1, owner, row, 0, NZ)
        else:
            m = (q - 8) % 8
            half, sd = m // 4, (m // 2) % 2
            x = lax.rem(chip_x + (X - 1 if sd == 0 else 1), X)
            owner = 2 * (x // 2) + (core if half == 0 else 1 - core)
            if q < 16:
                row_products(q, 2 - 2 * parity, owner, row, side_low, HALF)
            else:
                row_products(q, 2 * parity, owner, row, z_low, HALF)
    out[...] = 2.0 * held[0:ROWS] - acc[:, 0:NZ]


def products(where, table, density, own1, far, side, zrow):
    rows, nz, b, _ = density.shape
    anywhere = pl.BlockSpec(memory_space=pl.ANY)
    return pl.pallas_call(
        product_kernel,
        out_shape=jax.ShapeDtypeStruct(density.shape, density.dtype),
        grid_spec=pltpu.PrefetchScalarGridSpec(
            num_scalar_prefetch=2,
            grid=(),
            in_specs=[anywhere] * 5,
            out_specs=pl.BlockSpec(memory_space=pltpu.VMEM),
            scratch_shapes=[
                pltpu.VMEM((24, nz, b, b), density.dtype),
                pltpu.VMEM((rows, nz + 1, b, b), density.dtype),
                pltpu.SemaphoreType.DMA((24,)),
            ],
        ),
        compiler_params=pltpu.CompilerParams(vmem_limit_bytes=40 * 2**20),
    )(where, table, density, own1, far, side, zrow)


def shards(density, block_cols, targets):
    del targets
    own1, far, side, zrow, table = gather(density, block_cols)
    where = jnp.stack([lax.axis_index("blk"), lax.axis_index("inner")]).astype(jnp.int32)
    return products(where, table, density, own1, far, side, zrow)


def solution(mesh):
    return jax.shard_map(
        shards,
        mesh=mesh,
        in_specs=(
            P(("blk", "inner"), None, None, None),
            P(("blk", "inner"), None),
            P(("blk", "inner"), None, None),
        ),
        out_specs=P(("blk", "inner"), None, None, None),
        check_vma=False,
    )
```

```python
import functools

import jax
import jax.numpy as jnp
from jax import lax
from jax.experimental import pallas as pl
from jax.experimental.pallas import tpu as pltpu
from jax.sharding import PartitionSpec as P

MESH = pl.DeviceIdType.MESH
PER = 3
NZ = 9
HALF = 6
X = 4
ROWS = 2


def gather_kernel(
    den, cols, own1, far, side, zrow, table,
    side_s, side_r, far_s, far_r, z_s, z_r,
    mown_s, mown_r, mfar_s, mfar_r, mside_s, mside_r, mz_s, mz_r,
    cols_s, cols_r, local_s,
):
    blk = lax.axis_index("blk")
    inner = lax.axis_index("inner")
    strips = lax.axis_size("blk")
    parity = lax.rem(blk, 2)
    core = lax.rem(inner, 2)
    chip_x = 2 * (inner // 2) + parity

    def at_x(x):
        x = lax.rem(x, X)
        return (blk - parity + lax.rem(x, 2), 2 * (x // 2) + core)

    right, left = at_x(chip_x + 1), at_x(chip_x + X - 1)
    mirror = (blk, inner + 1 - 2 * core)
    z_to = (lax.rem(blk + strips + 2 - 4 * parity, strips), inner)
    z_from = (lax.rem(blk + strips - 2 + 4 * parity, strips), inner)

    def peer(offset, other):
        return (lax.rem(blk + offset + strips, strips), lax.rem(inner + other, 4))

    peers = [(o, i) for o in (-1, 0, 1) for i in range(4) if (o, i) != (0, 0)]
    barrier = pltpu.get_barrier_semaphore()
    for o, i in peers:
        pl.semaphore_signal(barrier, inc=1, device_id=peer(o, i), device_id_type=MESH)
    for device in (z_to, z_from):
        pl.semaphore_signal(barrier, inc=1, device_id=device, device_id_type=MESH)
    pl.semaphore_wait(barrier, len(peers) + 2)

    sent = []

    def send(src, dst, s, r, device):
        copy = pltpu.make_async_remote_copy(
            src_ref=src, dst_ref=dst, send_sem=s, recv_sem=r,
            device_id=device, device_id_type=MESH,
        )
        copy.start()
        sent.append(copy)

    def arrived(dst, r):
        pltpu.make_async_remote_copy(
            src_ref=dst, dst_ref=dst, send_sem=r, recv_sem=r,
            device_id=mirror, device_id_type=MESH,
        ).wait_recv()

    def groups(p):
        return (1, 2 * p, 2 - 2 * p)

    def slots(group):
        return pl.ds(PER * group, PER)

    mine = groups(parity)
    theirs = groups(1 - parity)
    z_place = (PER * parity, PER * (1 - parity))

    for n in range(6):
        g, row = n // 2, n % 2
        cut = slots(mine[g])
        for sd, device in ((0, right), (1, left)):
            send(den.at[row, cut], side.at[0, sd, row, cut],
                 side_s.at[sd, n], side_r.at[sd, n], device)
    for k, (o, i) in enumerate(peers):
        send(cols, table.at[1 - o, inner], cols_s.at[k], cols_r.at[1 - o, inner], peer(o, i))
    local = pltpu.make_async_copy(cols, table.at[1, inner], local_s)
    local.start()
    for n in range(6):
        g, row = n // 2, n % 2
        cut = slots(g)
        send(den.at[row, cut], own1.at[row, cut], mown_s.at[n], mown_r.at[n], mirror)

    def z_arrived(m):
        g, row, sd = m // 4, (m // 2) % 2, m % 2
        place = pl.ds(z_place[g], PER)
        arrived(zrow.at[0, sd, row, place], z_r.at[m])
        send(zrow.at[0, sd, row, place], zrow.at[1, sd, row, place],
             mz_s.at[m], mz_r.at[m], mirror)

    def far_arrived(j):
        for row in range(2):
            cut = slots(mine[j])
            arrived(far.at[0, row, cut], far_r.at[row, j])
            send(far.at[0, row, cut], far.at[1, row, cut],
                 mfar_s.at[row, j], mfar_r.at[row, j], mirror)

    for n in range(6):
        g, row = n // 2, n % 2
        cut = slots(theirs[g])
        for sd in range(2):
            arrived(side.at[0, sd, row, cut], side_r.at[sd, n])
            if g < 2:
                m = 2 * n + sd
                send(side.at[0, sd, row, cut],
                     zrow.at[0, sd, row, pl.ds(z_place[g], PER)],
                     z_s.at[m], z_r.at[m], z_to)
            if row == sd:
                send(side.at[0, sd, row, cut], far.at[0, row, cut],
                     far_s.at[row, g], far_r.at[row, g], (right, left)[sd])
            if g != 1:
                m = 2 * row + sd + (4 if g == 2 else 0)
                send(side.at[0, sd, row, cut], side.at[1, sd, row, cut],
                     mside_s.at[m], mside_r.at[m], mirror)
        if n >= 2:
            z_arrived(n - 2)
    far_arrived(0)
    z_arrived(4)
    z_arrived(5)
    far_arrived(1)
    z_arrived(6)
    z_arrived(7)
    far_arrived(2)

    for n in range(6):
        g, row = n // 2, n % 2
        arrived(own1.at[row, slots(g)], mown_r.at[n])
        arrived(far.at[1, row, slots(mine[g])], mfar_r.at[row, g])
        for sd in range(2):
            if g != 1:
                m = 2 * row + sd + (4 if g == 2 else 0)
                arrived(side.at[1, sd, row, slots(theirs[g])], mside_r.at[m])
            if g < 2:
                m = 2 * n + sd
                arrived(zrow.at[1, sd, row, pl.ds(z_place[g], PER)], mz_r.at[m])
    local.wait()
    for o, i in peers:
        other = lax.rem(inner + i, 4)
        arrived(table.at[1 + o, other], cols_r.at[1 + o, other])
    for copy in sent:
        copy.wait_send()


def gather(density, block_cols):
    rows, nz, b, _ = density.shape
    f32 = density.dtype
    dma = pltpu.SemaphoreType.DMA
    anywhere = pl.BlockSpec(memory_space=pl.ANY)
    return pl.pallas_call(
        gather_kernel,
        out_shape=(
            jax.ShapeDtypeStruct((rows, nz, b, b), f32),
            jax.ShapeDtypeStruct((2, rows, nz, b, b), f32),
            jax.ShapeDtypeStruct((2, 2, rows, nz, b, b), f32),
            jax.ShapeDtypeStruct((2, 2, rows, HALF, b, b), f32),
            jax.ShapeDtypeStruct((3, 4, rows, nz), jnp.int32),
        ),
        in_specs=[anywhere, anywhere],
        out_specs=(anywhere,) * 5,
        scratch_shapes=[
            dma((2, 6)), dma((2, 6)), dma((2, 3)), dma((2, 3)), dma((8,)), dma((8,)),
            dma((6,)), dma((6,)), dma((2, 3)), dma((2, 3)),
            dma((8,)), dma((8,)), dma((8,)), dma((8,)),
            dma((11,)), dma((3, 4)), dma,
        ],
        compiler_params=pltpu.CompilerParams(collective_id=0, has_side_effects=True),
    )(density, block_cols)


def product_kernel(
    where, table, den, own1, far, side, zrow, out,
    held, acc, sem,
):
    blk, inner = where[0], where[1]
    parity = lax.rem(blk, 2)
    chip_x = 2 * (inner // 2) + parity
    core = lax.rem(inner, 2)
    side_low = PER * parity
    z_low = PER * (1 - parity)

    def source(q):
        if q < 2:
            return den.at[q], held.at[q]
        if q < 4:
            return own1.at[q - 2], held.at[q]
        if q < 8:
            return far.at[(q - 4) // 2, q % 2], held.at[q]
        if q < 16:
            m = q - 8
            cut = pl.ds(side_low, HALF)
            return side.at[m // 4, (m // 2) % 2, m % 2, cut], held.at[q, cut]
        m = q - 16
        return zrow.at[m // 4, (m // 2) % 2, m % 2], held.at[q, pl.ds(z_low, HALF)]

    copies = [pltpu.make_async_copy(*source(q), sem.at[q]) for q in range(24)]
    for copy in copies:
        copy.start()
    acc[...] = jnp.zeros_like(acc)

    def split(value):
        high = value.astype(jnp.bfloat16)
        return high, (value - high.astype(jnp.float32)).astype(jnp.bfloat16)

    def row_products(q, offset, owner, row, first, count):
        group = 2 - offset
        for mine in range(ROWS):
            me = blk * (4 * ROWS) + inner * ROWS + mine
            slot = jnp.int32(-1)
            for a in range(PER):
                s = PER * group + a
                slot = jnp.where(table[offset, owner, row, s] == me, s, slot)

            @pl.when(slot >= 0)
            def _():
                left = held[q, slot].T
                left_high, left_low = split(left)
                lhs = jnp.concatenate([left_high, left_low, left_high], axis=1)
                for t in range(count):
                    right_high, right_low = split(held[q, first + t])
                    rhs = jnp.concatenate([right_high, right_high, right_low], axis=0)
                    product = jnp.dot(lhs, rhs, preferred_element_type=jnp.float32)
                    e = offset - 1 + (first + t) // PER
                    column = table[offset, owner, row, first + t]
                    place = jnp.int32(NZ)
                    for a in range(PER):
                        u = PER * e + a
                        place = jnp.where(table[1, inner, mine, u] == column, u, place)
                    acc[mine, place] += product

    for q in range(24):
        copies[q].wait()
        row = q % 2
        if q < 8:
            owner = (inner, inner + 1 - 2 * core, lax.rem(inner + 2, 4),
                     lax.rem(inner + 2, 4) + 1 - 2 * core)[q // 2]
            row_products(q, 1, owner, row, 0, NZ)
        else:
            m = (q - 8) % 8
            half, sd = m // 4, (m // 2) % 2
            x = lax.rem(chip_x + (X - 1 if sd == 0 else 1), X)
            owner = 2 * (x // 2) + (core if half == 0 else 1 - core)
            if q < 16:
                row_products(q, 2 - 2 * parity, owner, row, side_low, HALF)
            else:
                row_products(q, 2 * parity, owner, row, z_low, HALF)
    out[...] = 2.0 * held[0:ROWS] - acc[:, 0:NZ]


def products(where, table, density, own1, far, side, zrow):
    rows, nz, b, _ = density.shape
    anywhere = pl.BlockSpec(memory_space=pl.ANY)
    return pl.pallas_call(
        product_kernel,
        out_shape=jax.ShapeDtypeStruct(density.shape, density.dtype),
        grid_spec=pltpu.PrefetchScalarGridSpec(
            num_scalar_prefetch=2,
            grid=(),
            in_specs=[anywhere] * 5,
            out_specs=pl.BlockSpec(memory_space=pltpu.VMEM),
            scratch_shapes=[
                pltpu.VMEM((24, nz, b, b), density.dtype),
                pltpu.VMEM((rows, nz + 1, b, b), density.dtype),
                pltpu.SemaphoreType.DMA((24,)),
            ],
        ),
        compiler_params=pltpu.CompilerParams(vmem_limit_bytes=62 * 2**20),
    )(where, table, density, own1, far, side, zrow)


def shards(density, block_cols, targets):
    del targets
    own1, far, side, zrow, table = gather(density, block_cols)
    where = jnp.stack([lax.axis_index("blk"), lax.axis_index("inner")]).astype(jnp.int32)
    return products(where, table, density, own1, far, side, zrow)


def solution(mesh):
    return jax.shard_map(
        shards,
        mesh=mesh,
        in_specs=(
            P(("blk", "inner"), None, None, None),
            P(("blk", "inner"), None),
            P(("blk", "inner"), None, None),
        ),
        out_specs=P(("blk", "inner"), None, None, None),
        check_vma=False,
    )
```

```python
import jax
import jax.numpy as jnp
from jax import lax
from jax.experimental import pallas as pl
from jax.experimental.pallas import tpu as pltpu
from jax.sharding import PartitionSpec as P

MESH = pl.DeviceIdType.MESH
PER = 3
NZ = 9
X = 4
ROWS = 2


def split(value):
    high = value.astype(jnp.bfloat16)
    return high, (value - high.astype(jnp.float32)).astype(jnp.bfloat16)


def find(columns, wanted, places, otherwise):
    place = jnp.int32(otherwise)
    for column, here in zip(columns, places):
        place = jnp.where(column == wanted, here, place)
    return place


def left_side(blocks):
    highs, lows = zip(*(split(block.T) for block in blocks))
    return jnp.concatenate(highs + lows + highs, axis=1)


def right_side(columns_of_blocks):
    columns = []
    for blocks in columns_of_blocks:
        highs, lows = zip(*(split(block) for block in blocks))
        columns.append(jnp.concatenate(highs + highs + lows, axis=0))
    return jnp.concatenate(columns, axis=1)


def square_kernel(
    den, cols, out,
    own0, own1, side, za, zb0, zb1, fa, fb, fc,
    c_own, c_side, c_z, c_far, t_own, t_side, t_z, t_far,
    side_s, side_r, far_s, far_r, z_s, z_r,
    mown_s, mown_r, mfar_s, mfar_r, mside_s, mside_r, mz_s, mz_r,
    cs_s, cs_r, cz_s, cz_r, cf_s, cf_r, mc_s, mc_r, local_s, table_s,
):
    blk = lax.axis_index("blk")
    inner = lax.axis_index("inner")
    strips = lax.axis_size("blk")
    parity = lax.rem(blk, 2)
    core = lax.rem(inner, 2)
    chip_x = 2 * (inner // 2) + parity

    def at_x(x):
        x = lax.rem(x, X)
        return (blk - parity + lax.rem(x, 2), 2 * (x // 2) + core)

    right, left = at_x(chip_x + 1), at_x(chip_x + X - 1)
    mirror = (blk, inner + 1 - 2 * core)
    z_to = (lax.rem(blk + strips + 2 - 4 * parity, strips), inner)
    z_from = (lax.rem(blk + strips - 2 + 4 * parity, strips), inner)

    barrier = pltpu.get_barrier_semaphore()
    for device in (right, left, mirror, z_to, z_from):
        pl.semaphore_signal(barrier, inc=1, device_id=device, device_id_type=MESH)

    owned = []
    for row in range(ROWS):
        copy = pltpu.make_async_copy(den.at[row], own0.at[row, pl.ds(0, NZ)], local_s.at[row])
        copy.start()
        owned.append(copy)
    tables = [pltpu.make_async_copy(cols, t_own.at[0], table_s.at[0])]
    tables[0].start()

    none = jnp.zeros(den.shape[2:], jnp.float32)
    for row in range(ROWS):
        own0[row, NZ] = none
        own1[row, NZ] = none
        for half in range(2):
            for buffer in (fa, fb, fc):
                buffer[half, row, PER] = none
            for sd in range(2):
                side[half, sd, row, NZ] = none
                za[half, sd, row, PER] = none
                (zb0, zb1)[row][half, sd, PER] = none

    pl.semaphore_wait(barrier, 5)

    sent = []

    def send(src, dst, s, r, device):
        copy = pltpu.make_async_remote_copy(
            src_ref=src, dst_ref=dst, send_sem=s, recv_sem=r,
            device_id=device, device_id_type=MESH,
        )
        copy.start()
        sent.append(copy)

    def arrived(dst, r):
        pltpu.make_async_remote_copy(
            src_ref=dst, dst_ref=dst, send_sem=r, recv_sem=r,
            device_id=mirror, device_id_type=MESH,
        ).wait_recv()

    def groups(p):
        return (2 * p, 1, 2 - 2 * p)

    def slots(group):
        return pl.ds(PER * group, PER)

    three = pl.ds(0, PER)
    mine = groups(parity)
    theirs = groups(1 - parity)

    for sd, device in ((0, right), (1, left)):
        send(cols, c_side.at[0, sd], cs_s.at[sd], cs_r.at[sd], device)
    for n in range(6):
        g, row = n // 2, n % 2
        cut = slots(mine[g])
        for sd, device in ((0, right), (1, left)):
            send(den.at[row, cut], side.at[0, sd, row, cut],
                 side_s.at[sd, n], side_r.at[sd, n], device)
    send(cols, c_own, mc_s.at[0], mc_r.at[0], mirror)
    for row in range(ROWS):
        send(den.at[row], own1.at[row, pl.ds(0, NZ)], mown_s.at[row], mown_r.at[row], mirror)

    def load_table(k, src, dst):
        copy = pltpu.make_async_copy(src, dst, table_s.at[k])
        copy.start()
        tables.append(copy)

    def z_part(half, m):
        g, row, sd = m // 4, (m // 2) % 2, m % 2
        if g == 0:
            return za.at[half, sd, row, three]
        return (zb0, zb1)[row].at[half, sd, three]

    def z_arrived(m):
        arrived(z_part(0, m), z_r.at[m])
        send(z_part(0, m), z_part(1, m), mz_s.at[m], mz_r.at[m], mirror)

    def far_part(half, row, g):
        return (fa, fb, fc)[g].at[half, row, three]

    def far_arrived(g):
        for row in range(ROWS):
            arrived(far_part(0, row, g), far_r.at[row, g])
            send(far_part(0, row, g), far_part(1, row, g),
                 mfar_s.at[row, g], mfar_r.at[row, g], mirror)

    def side_arrived(n):
        g, row = n // 2, n % 2
        cut = slots(theirs[g])
        for sd in range(2):
            here = side.at[0, sd, row, cut]
            arrived(here, side_r.at[sd, n])
            if g < 2:
                m = 2 * n + sd
                send(here, z_part(0, m), z_s.at[m], z_r.at[m], z_to)
            if row == sd:
                send(here, far_part(0, row, g), far_s.at[row, g], far_r.at[row, g],
                     (right, left)[sd])
            if g > 0:
                m = 4 * (g - 1) + 2 * row + sd
                send(here, side.at[1, sd, row, cut], mside_s.at[m], mside_r.at[m], mirror)

    first = blk * (4 * ROWS) + inner * ROWS

    def wanted(i, group):
        return [t_own[0, i, PER * group + b] for b in range(PER)]

    def add(i, lhs, e, rhs, fresh=False):
        product = jnp.dot(lhs, rhs, preferred_element_type=jnp.float32)
        width = den.shape[3]
        for b in range(PER):
            part = product[:, b * width:(b + 1) * width]
            if fresh:
                out[i, PER * e + b] = part
            else:
                out[i, PER * e + b] += part

    def rights(rows, i, e):
        return right_side([
            [read(find(columns, want, places, empty)) for columns, places, empty, read in rows]
            for want in wanted(i, e)
        ])

    def own_products(buffer, half, fresh):
        def body(i, carry):
            lhs = left_side([
                buffer[row, find([t_own[half, row, PER + a] for a in range(PER)],
                                 first + i, range(PER, 2 * PER), PER)]
                for row in range(ROWS)
            ])
            present = [
                find([t_own[half, row, PER + a] for a in range(PER)], first + i, (1, 1, 1), 0)
                for row in range(ROWS)
            ]
            for e in range(3):
                rows = [
                    ([jnp.where(present[row] == 1, t_own[half, row, PER * e + b], -1)
                      for b in range(PER)],
                     range(PER * e, PER * e + PER), NZ,
                     lambda s, row=row: buffer[row, s])
                    for row in range(ROWS)
                ]
                add(i, lhs, e, rights(rows, i, e), fresh)
            return carry
        lax.fori_loop(0, ROWS, body, 0)

    def general(units, table, row_set, left_group, left_read, parts):
        def body(step, carry):
            unit, i = step // ROWS, lax.rem(step, ROWS)
            lefts, present = [], []
            for row in row_set:
                names = [table(unit, row, PER * left_group + a) for a in range(PER)]
                lefts.append(left_read(unit, row, find(names, first + i, range(PER), 0)))
                present.append(find(names, first + i, (1, 1, 1), 0))
            lhs = left_side(lefts)
            for group, e, read, base, empty in parts:
                rows = [
                    ([jnp.where(present[k] == 1, table(unit, row, PER * group + b), -1)
                      for b in range(PER)],
                     [base + b for b in range(PER)], empty,
                     lambda s, row=row: read(unit, row, s))
                    for k, row in enumerate(row_set)
                ]
                add(i, lhs, e, rights(rows, i, e))
            return carry
        lax.fori_loop(0, units * ROWS, body, 0)

    both = tuple(range(ROWS))

    def side_products():
        name = lambda u, row, s: t_side[u // 2, lax.rem(u, 2), row, s]
        read = lambda u, row, s: side[u // 2, lax.rem(u, 2), row, s]
        low = 2 * parity
        general(4, name, both, low, lambda u, row, a: read(u, row, PER * low + a),
                [(low, 1, read, PER * low, NZ), (1, 2 - 2 * parity, read, PER, NZ)])

    z_name = lambda u, row, s: t_z[u // 2, lax.rem(u, 2), row, s]
    z_left = lambda u, row, a: za[u // 2, lax.rem(u, 2), row, a]

    def za_products():
        general(4, z_name, both, 2 - 2 * parity, z_left,
                [(2 - 2 * parity, 1, z_left, 0, PER)])

    def zb_products(row):
        buffer = (zb0, zb1)[row]
        general(4, z_name, (row,), 2 - 2 * parity, z_left,
                [(1, 2 * parity, lambda u, _, s: buffer[u // 2, lax.rem(u, 2), s], 0, PER)])

    far_name = lambda u, row, s: t_far[u, row, s]
    far_left = lambda u, row, a: fb[u, row, a]

    def far_products(which):
        parts = []
        for g in which:
            buffer = (fa, fb, fc)[g]
            parts.append((mine[g], mine[g], lambda u, row, s, buffer=buffer: buffer[u, row, s],
                          0, PER))
        general(2, far_name, both, 1, far_left, parts)

    for copy in owned:
        copy.wait()
    tables[0].wait()
    own_products(own0, 0, True)

    for sd in range(2):
        arrived(c_side.at[0, sd], cs_r.at[sd])
        send(c_side.at[0, sd], c_z.at[0, sd], cz_s.at[sd], cz_r.at[sd], z_to)
        send(c_side.at[0, sd], c_side.at[1, sd], mc_s.at[1 + sd], mc_r.at[1 + sd], mirror)
    send(c_side.at[0, 0], c_far.at[0], cf_s.at[0], cf_r.at[0], right)
    side_arrived(0)
    arrived(c_own, mc_r.at[0])
    load_table(1, c_own, t_own.at[1])
    for row in range(ROWS):
        arrived(own1.at[row, pl.ds(0, NZ)], mown_r.at[row])
    tables[1].wait()
    own_products(own1, 1, False)
    side_arrived(1)
    arrived(c_far.at[0], cf_r.at[0])
    send(c_far.at[0], c_far.at[1], mc_s.at[3], mc_r.at[3], mirror)
    for sd in range(2):
        arrived(c_z.at[0, sd], cz_r.at[sd])
        send(c_z.at[0, sd], c_z.at[1, sd], mc_s.at[4 + sd], mc_r.at[4 + sd], mirror)
    side_arrived(2)
    z_arrived(0)
    for sd in range(2):
        arrived(c_side.at[1, sd], mc_r.at[1 + sd])
        arrived(c_z.at[1, sd], mc_r.at[4 + sd])
    arrived(c_far.at[1], mc_r.at[3])
    load_table(2, c_side, t_side)
    load_table(3, c_z, t_z)
    load_table(4, c_far, t_far)
    side_arrived(3)
    z_arrived(1)
    side_arrived(4)
    z_arrived(2)
    side_arrived(5)
    z_arrived(3)
    for k in (2, 3, 4):
        tables[k].wait()
    for n in range(2, 6):
        g, row = n // 2, n % 2
        for sd in range(2):
            arrived(side.at[1, sd, row, slots(theirs[g])], mside_r.at[4 * (g - 1) + 2 * row + sd])
    z_arrived(4)
    side_products()
    far_arrived(0)
    z_arrived(5)
    for m in range(4):
        arrived(z_part(1, m), mz_r.at[m])
    za_products()
    z_arrived(6)
    far_arrived(1)
    for m in (4, 5):
        arrived(z_part(1, m), mz_r.at[m])
    zb_products(0)
    for g in (0, 1):
        for row in range(ROWS):
            arrived(far_part(1, row, g), mfar_r.at[row, g])
    far_products((0, 1))
    z_arrived(7)
    far_arrived(2)
    for m in (6, 7):
        arrived(z_part(1, m), mz_r.at[m])
    zb_products(1)
    for row in range(ROWS):
        arrived(far_part(1, row, 2), mfar_r.at[row, 2])
    far_products((2,))
    for copy in sent:
        copy.wait_send()


def square_rows(density, block_cols):
    rows, nz, b, _ = density.shape
    f32, i32 = density.dtype, jnp.int32
    dma = pltpu.SemaphoreType.DMA
    anywhere = pl.BlockSpec(memory_space=pl.ANY)
    vmem, smem = pltpu.VMEM, pltpu.SMEM
    tables = [(rows, nz), (2, 2, rows, nz), (2, 2, rows, nz), (2, rows, nz)]
    return pl.pallas_call(
        square_kernel,
        out_shape=jax.ShapeDtypeStruct(density.shape, f32),
        in_specs=[anywhere, anywhere],
        out_specs=pl.BlockSpec(memory_space=pltpu.VMEM),
        scratch_shapes=[
            vmem((rows, nz + 1, b, b), f32), vmem((rows, nz + 1, b, b), f32),
            vmem((2, 2, rows, nz + 1, b, b), f32),
            vmem((2, 2, rows, PER + 1, b, b), f32),
            vmem((2, 2, PER + 1, b, b), f32), vmem((2, 2, PER + 1, b, b), f32),
            *[vmem((2, rows, PER + 1, b, b), f32)] * 3,
            *[vmem(shape, i32) for shape in tables],
            smem((2, rows, nz), i32), *[smem(shape, i32) for shape in tables[1:]],
            dma((2, 6)), dma((2, 6)), dma((2, 3)), dma((2, 3)), dma((8,)), dma((8,)),
            dma((2,)), dma((2,)), dma((2, 3)), dma((2, 3)),
            dma((8,)), dma((8,)), dma((8,)), dma((8,)),
            dma((2,)), dma((2,)), dma((2,)), dma((2,)), dma((1,)), dma((1,)),
            dma((6,)), dma((6,)), dma((2,)), dma((5,)),
        ],
        compiler_params=pltpu.CompilerParams(
            collective_id=0, has_side_effects=True, vmem_limit_bytes=60 * 2**20),
    )(density, block_cols)


def shards(density, block_cols, targets):
    del targets
    return 2.0 * density - square_rows(density, block_cols)


def solution(mesh):
    return jax.shard_map(
        shards,
        mesh=mesh,
        in_specs=(
            P(("blk", "inner"), None, None, None),
            P(("blk", "inner"), None),
            P(("blk", "inner"), None, None),
        ),
        out_specs=P(("blk", "inner"), None, None, None),
        check_vma=False,
    )
```

```python
import jax
import jax.numpy as jnp
from jax import lax
from jax.experimental import pallas as pl
from jax.experimental.pallas import tpu as pltpu
from jax.sharding import PartitionSpec as P

MESH = pl.DeviceIdType.MESH
PER = 3
NZ = 9
X = 4
ROWS = 2
SIDE = ((0, 0, 0, 1), (0, 0, 1, 2), (1, 0, 0, 3), (0, 1, 0, 3), (1, 1, 0, 3), (0, 2, 0, 3), (1, 2, 0, 3))


def split(value):
    high = value.astype(jnp.bfloat16)
    return high, (value - high.astype(jnp.float32)).astype(jnp.bfloat16)


def find(columns, wanted, places, otherwise):
    place = jnp.int32(otherwise)
    for column, here in zip(columns, places):
        place = jnp.where(column == wanted, here, place)
    return place


def left_side(blocks):
    highs, lows = zip(*(split(block.T) for block in blocks))
    return jnp.concatenate(highs + lows + highs, axis=1)


def right_side(columns_of_blocks):
    columns = []
    for blocks in columns_of_blocks:
        highs, lows = zip(*(split(block) for block in blocks))
        columns.append(jnp.concatenate(highs + highs + lows, axis=0))
    return jnp.concatenate(columns, axis=1)


def square_kernel(
    den, cols, out,
    own0, own1, side, za, zb0, zb1, fa, fb, fc,
    lz, lf, c_own, c_side, c_z, c_far, t_own, t_side, t_z, t_far,
    side_s, side_r, far_s, far_r, z_s, z_r,
    mown_s, mown_r, mfar_s, mfar_r, mside_s, mside_r, mz_s, mz_r,
    cs_s, cs_r, cz_s, cz_r, cf_s, cf_r, mc_s, mc_r, local_s, table_s,
):
    blk = lax.axis_index("blk")
    inner = lax.axis_index("inner")
    strips = lax.axis_size("blk")
    parity = lax.rem(blk, 2)
    core = lax.rem(inner, 2)
    chip_x = 2 * (inner // 2) + parity

    def at_x(x):
        x = lax.rem(x, X)
        return (blk - parity + lax.rem(x, 2), 2 * (x // 2) + core)

    right, left = at_x(chip_x + 1), at_x(chip_x + X - 1)
    far = at_x(chip_x + 2)
    mirror = (blk, inner + 1 - 2 * core)
    z_to = (lax.rem(blk + strips + 2 - 4 * parity, strips), inner)
    z_from = (lax.rem(blk + strips - 2 + 4 * parity, strips), inner)

    barrier = pltpu.get_barrier_semaphore()
    for device in (right, left, far, mirror, z_to, z_from):
        pl.semaphore_signal(barrier, inc=1, device_id=device, device_id_type=MESH)

    owned = []
    for row in range(ROWS):
        copy = pltpu.make_async_copy(den.at[row], own0.at[row, pl.ds(0, NZ)], local_s.at[row])
        copy.start()
        owned.append(copy)
    tables = [pltpu.make_async_copy(cols, t_own.at[0], table_s.at[0])]
    tables[0].start()

    none = jnp.zeros(den.shape[2:], jnp.float32)
    for row in range(ROWS):
        own0[row, NZ] = none
        own1[row, NZ] = none
        for half in range(2):
            for buffer in (fa, fb, fc):
                buffer[half, row, PER] = none
            for sd in range(2):
                side[half, sd, row, NZ] = none
                za[half, sd, row, PER] = none
                (zb0, zb1)[row][half, sd, PER] = none

    pl.semaphore_wait(barrier, 6)

    sent = []

    def send(src, dst, s, r, device):
        copy = pltpu.make_async_remote_copy(
            src_ref=src, dst_ref=dst, send_sem=s, recv_sem=r,
            device_id=device, device_id_type=MESH,
        )
        copy.start()
        sent.append(copy)

    def arrived(dst, r):
        pltpu.make_async_remote_copy(
            src_ref=dst, dst_ref=dst, send_sem=r, recv_sem=r,
            device_id=mirror, device_id_type=MESH,
        ).wait_recv()

    def groups(p):
        return (2 * p, 1, 2 - 2 * p)

    def slots(group, first=0, count=PER):
        return pl.ds(PER * group + first, count)

    three = pl.ds(0, PER)
    mine = groups(parity)
    theirs = groups(1 - parity)

    for sd, device in ((0, right), (1, left)):
        send(cols, c_side.at[0, sd], cs_s.at[sd], cs_r.at[sd], device)
    send(cols, c_far.at[0], cf_s.at[0], cf_r.at[0], far)
    for n, (row, g, low, count) in enumerate(SIDE):
        cut = slots(mine[g], low, count)
        for sd, device in ((0, right), (1, left)):
            send(den.at[row, cut], side.at[0, sd, row, cut],
                 side_s.at[sd, n], side_r.at[sd, n], device)
    send(cols, c_own, mc_s.at[0], mc_r.at[0], mirror)
    for row in range(ROWS):
        send(den.at[row], own1.at[row, pl.ds(0, NZ)], mown_s.at[row], mown_r.at[row], mirror)

    def load_table(k, src, dst):
        copy = pltpu.make_async_copy(src, dst, table_s.at[k])
        copy.start()
        tables.append(copy)

    def z_part(half, sd, piece):
        row, g, low, count = piece
        cut = pl.ds(low, count)
        return za.at[half, sd, row, cut] if g == 0 else (zb0, zb1)[row].at[half, sd, cut]

    z_pieces = [(n, sd) for n, piece in enumerate(SIDE) if piece[1] < 2 for sd in range(2)]

    def z_arrived(m):
        n, sd = z_pieces[m]
        piece = SIDE[n]
        arrived(z_part(0, sd, piece), z_r.at[m])
        send(z_part(0, sd, piece), z_part(1, sd, piece), mz_s.at[m], mz_r.at[m], mirror)

    def z_mirrored(m):
        n, sd = z_pieces[m]
        arrived(z_part(1, sd, SIDE[n]), mz_r.at[m])

    def far_part(half, piece):
        row, g, low, count = piece
        return (fa, fb, fc)[g].at[half, row, pl.ds(low, count)]

    def far_pieces(piece):
        row, g, low, count = piece
        return [piece] if g < 2 else [(row, g, 0, 2), (row, g, 2, 1)]

    far_list = [(row, k, piece) for row in range(ROWS) for k, piece in
                enumerate(p for q in SIDE if q[0] == row for p in far_pieces(q))]

    def far_wait(half, g, sems, row, last=None):
        for r, k, piece in far_list:
            if r == row and piece[1] == g and (last is None or last == (piece[2] == 2)):
                arrived(far_part(half, piece), sems.at[r, k])
                if half == 0:
                    send(far_part(0, piece), far_part(1, piece),
                         mfar_s.at[r, k], mfar_r.at[r, k], mirror)

    def far_arrived(g, last=None):
        for row in range(ROWS):
            far_wait(0, g, far_r, row, last)

    def far_mirrored(g):
        for row in range(ROWS):
            far_wait(1, g, mfar_r, row)

    def side_arrived(n):
        row, g, low, count = SIDE[n]
        for sd in range(2):
            here = side.at[0, sd, row, slots(theirs[g], low, count)]
            arrived(here, side_r.at[sd, n])
            if g < 2:
                m = 2 * n + sd
                send(here, z_part(0, sd, SIDE[n]), z_s.at[m], z_r.at[m], z_to)
            if row == sd:
                for r, k, piece in far_list:
                    if r == row and piece in far_pieces(SIDE[n]):
                        there = side.at[0, sd, row, slots(theirs[g], piece[2], piece[3])]
                        send(there, far_part(0, piece), far_s.at[row, k], far_r.at[row, k],
                             (right, left)[sd])
            if g > 0:
                send(here, side.at[1, sd, row, slots(theirs[g], low, count)],
                     mside_s.at[sd, n], mside_r.at[sd, n], mirror)

    def side_mirrored():
        for n, (row, g, low, count) in enumerate(SIDE):
            if g > 0:
                for sd in range(2):
                    arrived(side.at[1, sd, row, slots(theirs[g], low, count)], mside_r.at[sd, n])

    first = blk * (4 * ROWS) + inner * ROWS

    def wanted(i, group):
        return [t_own[0, i, PER * group + b] for b in range(PER)]

    def add(i, lhs, e, rhs, fresh=False):
        product = jnp.dot(lhs, rhs, preferred_element_type=jnp.float32)
        width = den.shape[3]
        for b in range(PER):
            part = product[:, b * width:(b + 1) * width]
            if fresh:
                out[i, PER * e + b] = part
            else:
                out[i, PER * e + b] += part

    def rights(rows, i, e):
        return right_side([
            [read(find(columns, want, places, empty)) for columns, places, empty, read in rows]
            for want in wanted(i, e)
        ])

    def own_products(buffer, half, fresh):
        def body(i, carry):
            lhs = left_side([
                buffer[row, find([t_own[half, row, PER + a] for a in range(PER)],
                                 first + i, range(PER, 2 * PER), PER)]
                for row in range(ROWS)
            ])
            present = [
                find([t_own[half, row, PER + a] for a in range(PER)], first + i, (1, 1, 1), 0)
                for row in range(ROWS)
            ]
            for e in range(3):
                rows = [
                    ([jnp.where(present[row] == 1, t_own[half, row, PER * e + b], -1)
                      for b in range(PER)],
                     range(PER * e, PER * e + PER), NZ,
                     lambda s, row=row: buffer[row, s])
                    for row in range(ROWS)
                ]
                add(i, lhs, e, rights(rows, i, e), fresh)
            return carry
        lax.fori_loop(0, ROWS, body, 0)

    def lefts(names, reads, i):
        return left_side([read(find(name, first + i, range(PER), 0))
                          for name, read in zip(names, reads)])

    def guarded(name, columns, i):
        present = find(name, first + i, (1, 1, 1), 0) == 1
        return [jnp.where(present, column, -1) for column in columns]

    def entries(table, index, group):
        return [table[(*index, PER * group + b)] for b in range(PER)]

    two = [(half, sd) for half in range(2) for sd in range(2)]
    pair = [(half, row) for half in range(2) for row in range(ROWS)]

    def side_products(i):
        low = 2 * parity
        for row in range(ROWS):
            names = [entries(t_side, (h, sd, row), low) for h, sd in two]
            reads = [lambda s, h=h, sd=sd: side[h, sd, row, s] for h, sd in two]
            lhs = lefts(names, [lambda a, r=r: r(PER * low + a) for r in reads], i)
            for group, e in ((low, 1), (1, 2 - 2 * parity)):
                rows = [(guarded(name, entries(t_side, (h, sd, row), group), i),
                         [PER * group + b for b in range(PER)], NZ, read)
                        for name, (h, sd), read in zip(names, two, reads)]
                add(i, lhs, e, rights(rows, i, e))

    z_group = 2 - 2 * parity

    def z_lefts(i):
        for row in range(ROWS):
            names = [entries(t_z, (h, sd, row), z_group) for h, sd in two]
            reads = [lambda s, h=h, sd=sd: za[h, sd, row, s] for h, sd in two]
            lz[row, i] = lefts(names, reads, i)

    def z_products(row, group, e, read, i):
        rows = [(guarded(entries(t_z, (h, sd, row), z_group), entries(t_z, (h, sd, row), group), i),
                 range(PER), PER, lambda s, h=h, sd=sd: read(h, sd, s))
                for h, sd in two]
        add(i, lz[row, i], e, rights(rows, i, e))

    def za_products(i):
        for row in range(ROWS):
            z_products(row, z_group, 1, lambda h, sd, s: za[h, sd, row, s], i)

    def zb_products(row, i):
        buffer = (zb0, zb1)[row]
        z_products(row, 1, 2 * parity, lambda h, sd, s: buffer[h, sd, s], i)

    def far_lefts(i):
        names = [entries(t_far, (h, row), 1) for h, row in pair]
        reads = [lambda s, h=h, row=row: fb[h, row, s] for h, row in pair]
        lf[i] = lefts(names, reads, i)

    def far_products(g, i):
        buffer, group = (fa, fb, fc)[g], mine[g]
        rows = [(guarded(entries(t_far, (h, row), 1), entries(t_far, (h, row), group), i),
                 range(PER), PER, lambda s, h=h, row=row: buffer[h, row, s])
                for h, row in pair]
        add(i, lf[i], group, rights(rows, i, group))

    def each_row(*steps):
        def body(i, carry):
            for step in steps:
                step(i)
            return carry
        lax.fori_loop(0, ROWS, body, 0)

    for copy in owned:
        copy.wait()
    tables[0].wait()
    own_products(own0, 0, True)

    for sd in range(2):
        arrived(c_side.at[0, sd], cs_r.at[sd])
        send(c_side.at[0, sd], c_z.at[0, sd], cz_s.at[sd], cz_r.at[sd], z_to)
        send(c_side.at[0, sd], c_side.at[1, sd], mc_s.at[1 + sd], mc_r.at[1 + sd], mirror)
    side_arrived(0)
    side_arrived(1)
    arrived(c_own, mc_r.at[0])
    load_table(1, c_own, t_own.at[1])
    for row in range(ROWS):
        arrived(own1.at[row, pl.ds(0, NZ)], mown_r.at[row])
    tables[1].wait()
    own_products(own1, 1, False)
    side_arrived(2)
    arrived(c_far.at[0], cf_r.at[0])
    send(c_far.at[0], c_far.at[1], mc_s.at[3], mc_r.at[3], mirror)
    for sd in range(2):
        arrived(c_z.at[0, sd], cz_r.at[sd])
        send(c_z.at[0, sd], c_z.at[1, sd], mc_s.at[4 + sd], mc_r.at[4 + sd], mirror)
    side_arrived(3)
    z_arrived(0)
    z_arrived(1)
    for sd in range(2):
        arrived(c_side.at[1, sd], mc_r.at[1 + sd])
        arrived(c_z.at[1, sd], mc_r.at[4 + sd])
    arrived(c_far.at[1], mc_r.at[3])
    load_table(2, c_side, t_side)
    load_table(3, c_z, t_z)
    load_table(4, c_far, t_far)
    side_arrived(4)
    z_arrived(2)
    z_arrived(3)
    side_arrived(5)
    z_arrived(4)
    side_arrived(6)
    z_arrived(5)
    for k in (2, 3, 4):
        tables[k].wait()
    side_mirrored()
    each_row(side_products)
    z_arrived(6)
    far_arrived(0)
    z_arrived(7)
    for m in range(6):
        z_mirrored(m)
    each_row(z_lefts, za_products)
    z_arrived(8)
    far_arrived(1)
    for m in (6, 7):
        z_mirrored(m)
    each_row(lambda i: zb_products(0, i))
    for g in (0, 1):
        far_mirrored(g)
    each_row(far_lefts, lambda i: far_products(0, i), lambda i: far_products(1, i))
    z_arrived(9)
    far_arrived(2, False)
    for m in (8, 9):
        z_mirrored(m)
    for i in range(ROWS):
        zb_products(1, i)
    far_arrived(2, True)
    far_mirrored(2)
    for i in range(ROWS):
        far_products(2, i)
    for copy in sent:
        copy.wait_send()


def square_rows(density, block_cols):
    rows, nz, b, _ = density.shape
    f32, i32 = density.dtype, jnp.int32
    dma = pltpu.SemaphoreType.DMA
    anywhere = pl.BlockSpec(memory_space=pl.ANY)
    vmem, smem = pltpu.VMEM, pltpu.SMEM
    tables = [(rows, nz), (2, 2, rows, nz), (2, 2, rows, nz), (2, rows, nz)]
    return pl.pallas_call(
        square_kernel,
        out_shape=jax.ShapeDtypeStruct(density.shape, f32),
        in_specs=[anywhere, anywhere],
        out_specs=pl.BlockSpec(memory_space=pltpu.VMEM),
        scratch_shapes=[
            vmem((rows, nz + 1, b, b), f32), vmem((rows, nz + 1, b, b), f32),
            vmem((2, 2, rows, nz + 1, b, b), f32),
            vmem((2, 2, rows, PER + 1, b, b), f32),
            vmem((2, 2, PER + 1, b, b), f32), vmem((2, 2, PER + 1, b, b), f32),
            *[vmem((2, rows, PER + 1, b, b), f32)] * 3,
            vmem((rows, rows, b, 12 * b), jnp.bfloat16), vmem((rows, b, 12 * b), jnp.bfloat16),
            *[vmem(shape, i32) for shape in tables],
            smem((2, rows, nz), i32), *[smem(shape, i32) for shape in tables[1:]],
            dma((2, 7)), dma((2, 7)), dma((2, 5)), dma((2, 5)), dma((10,)), dma((10,)),
            dma((2,)), dma((2,)), dma((2, 5)), dma((2, 5)),
            dma((2, 7)), dma((2, 7)), dma((10,)), dma((10,)),
            dma((2,)), dma((2,)), dma((2,)), dma((2,)), dma((1,)), dma((1,)),
            dma((6,)), dma((6,)), dma((2,)), dma((5,)),
        ],
        compiler_params=pltpu.CompilerParams(
            collective_id=0, has_side_effects=True, vmem_limit_bytes=60 * 2**20),
    )(density, block_cols)


def shards(density, block_cols, targets):
    del targets
    return 2.0 * density - square_rows(density, block_cols)


def solution(mesh):
    return jax.shard_map(
        shards,
        mesh=mesh,
        in_specs=(
            P(("blk", "inner"), None, None, None),
            P(("blk", "inner"), None),
            P(("blk", "inner"), None, None),
        ),
        out_specs=P(("blk", "inner"), None, None, None),
        check_vma=False,
    )
```

```python
import jax
import jax.numpy as jnp
from jax import lax
from jax.experimental import pallas as pl
from jax.experimental.pallas import tpu as pltpu
from jax.sharding import PartitionSpec as P

MESH = pl.DeviceIdType.MESH
PER = 3
NZ = 9
X = 4
ROWS = 2
SIDE = ((0, 0, 0, 1), (0, 0, 1, 2), (1, 0, 0, 3), (0, 1, 0, 3), (1, 1, 0, 3), (0, 2, 0, 3), (1, 2, 0, 3))


def split(value):
    high = value.astype(jnp.bfloat16)
    return high, (value - high.astype(jnp.float32)).astype(jnp.bfloat16)


def find(columns, wanted, places, otherwise):
    place = jnp.int32(otherwise)
    for column, here in zip(columns, places):
        place = jnp.where(column == wanted, here, place)
    return place


def left_side(blocks):
    highs, lows = zip(*(split(block.T) for block in blocks))
    return jnp.concatenate(highs + lows + highs, axis=1)


def right_side(columns_of_blocks):
    columns = []
    for blocks in columns_of_blocks:
        highs, lows = zip(*(split(block) for block in blocks))
        columns.append(jnp.concatenate(highs + highs + lows, axis=0))
    return jnp.concatenate(columns, axis=1)


def square_kernel(
    den, cols, out,
    own0, own1, side0, side1, side2, za, fa, fb, x_out, x_in, z_out, z_in,
    lf, c_own, c_side, c_z, c_far, c_next, t_own, t_side, t_z, t_far, t_next,
    side_s, side_r, far_s, far_r, z_s, z_r,
    mown_s, mown_r, mfar_s, mfar_r, mside_s, mside_r, mz_s, mz_r,
    cs_s, cs_r, cz_s, cz_r, cf_s, cf_r, cn_s, cn_r, mc_s, mc_r,
    xp_s, xp_r, zp_s, zp_r, local_s, table_s,
):
    blk = lax.axis_index("blk")
    inner = lax.axis_index("inner")
    strips = lax.axis_size("blk")
    parity = lax.rem(blk, 2)
    core = lax.rem(inner, 2)
    chip_x = 2 * (inner // 2) + parity

    def at_x(x):
        x = lax.rem(x, X)
        return (blk - parity + lax.rem(x, 2), 2 * (x // 2) + core)

    right, left = at_x(chip_x + 1), at_x(chip_x + X - 1)
    far = at_x(chip_x + 2)
    mirror = (blk, inner + 1 - 2 * core)
    z_to = (lax.rem(blk + strips + 2 - 4 * parity, strips), inner)
    z_from = (lax.rem(blk + strips - 2 + 4 * parity, strips), inner)

    barrier = pltpu.get_barrier_semaphore()
    for device in (right, left, far, mirror, z_to, z_from):
        pl.semaphore_signal(barrier, inc=1, device_id=device, device_id_type=MESH)

    owned = []
    for row in range(ROWS):
        copy = pltpu.make_async_copy(den.at[row], own0.at[row, pl.ds(0, NZ)], local_s.at[row])
        copy.start()
        owned.append(copy)
    tables = [pltpu.make_async_copy(cols, t_own.at[0], table_s.at[0])]
    tables[0].start()

    none = jnp.zeros(den.shape[2:], jnp.float32)
    for row in range(ROWS):
        own0[row, NZ] = none
        own1[row, NZ] = none
        for half in range(2):
            for buffer in (fa, fb):
                buffer[half, row, PER] = none
            for sd in range(2):
                for buffer in (side0, side1, side2):
                    buffer[half, sd, row, PER] = none
                za[half, sd, row, PER] = none

    pl.semaphore_wait(barrier, 6)

    sent = []

    def send(src, dst, s, r, device):
        copy = pltpu.make_async_remote_copy(
            src_ref=src, dst_ref=dst, send_sem=s, recv_sem=r,
            device_id=device, device_id_type=MESH,
        )
        copy.start()
        sent.append(copy)

    def arrived(dst, r):
        pltpu.make_async_remote_copy(
            src_ref=dst, dst_ref=dst, send_sem=r, recv_sem=r,
            device_id=mirror, device_id_type=MESH,
        ).wait_recv()

    def groups(p):
        return (2 * p, 1, 2 - 2 * p)

    def slots(group, first=0, count=PER):
        return pl.ds(PER * group + first, count)

    three = pl.ds(0, PER)
    mine = groups(parity)
    theirs = groups(1 - parity)

    def side_part(half, sd, piece):
        row, g, low, count = piece
        return (side0, side1, side2)[g].at[half, sd, row, pl.ds(low, count)]

    for sd, device in ((0, right), (1, left)):
        send(cols, c_side.at[0, sd], cs_s.at[sd], cs_r.at[sd], device)
    send(cols, c_far.at[0], cf_s.at[0], cf_r.at[0], far)
    send(cols, c_next, cn_s.at[0], cn_r.at[0], z_from)
    for n, (row, g, low, count) in enumerate(SIDE):
        cut = slots(mine[g], low, count)
        for sd, device in ((0, right), (1, left)):
            send(den.at[row, cut], side_part(0, sd, SIDE[n]),
                 side_s.at[sd, n], side_r.at[sd, n], device)
    send(cols, c_own, mc_s.at[0], mc_r.at[0], mirror)
    for row in range(ROWS):
        send(den.at[row], own1.at[row, pl.ds(0, NZ)], mown_s.at[row], mown_r.at[row], mirror)

    def load_table(k, src, dst):
        copy = pltpu.make_async_copy(src, dst, table_s.at[k])
        copy.start()
        tables.append(copy)

    def z_part(half, sd, piece):
        row, g, low, count = piece
        return za.at[half, sd, row, pl.ds(low, count)]

    z_pieces = [(n, sd) for n, piece in enumerate(SIDE) if piece[1] == 0 for sd in range(2)]

    def z_arrived(m):
        n, sd = z_pieces[m]
        piece = SIDE[n]
        arrived(z_part(0, sd, piece), z_r.at[m])
        send(z_part(0, sd, piece), z_part(1, sd, piece), mz_s.at[m], mz_r.at[m], mirror)

    def z_mirrored(m):
        n, sd = z_pieces[m]
        arrived(z_part(1, sd, SIDE[n]), mz_r.at[m])

    def far_part(half, piece):
        row, g, low, count = piece
        return (fa, fb)[g].at[half, row, pl.ds(low, count)]

    far_list = [(row, k, piece) for row in range(ROWS) for k, piece in
                enumerate(p for p in SIDE if p[0] == row and p[1] < 2)]

    def far_arrived(g):
        for row, k, piece in far_list:
            if piece[1] == g:
                arrived(far_part(0, piece), far_r.at[row, k])
                send(far_part(0, piece), far_part(1, piece),
                     mfar_s.at[row, k], mfar_r.at[row, k], mirror)

    def far_mirrored(g):
        for row, k, piece in far_list:
            if piece[1] == g:
                arrived(far_part(1, piece), mfar_r.at[row, k])

    def side_arrived(n):
        row, g, low, count = SIDE[n]
        for sd in range(2):
            here = side_part(0, sd, SIDE[n])
            arrived(here, side_r.at[sd, n])
            if g == 0:
                m = 2 * n + sd
                send(here, z_part(0, sd, SIDE[n]), z_s.at[m], z_r.at[m], z_to)
            for r, k, piece in far_list:
                if row == sd and piece == SIDE[n]:
                    send(here, far_part(0, piece), far_s.at[row, k], far_r.at[row, k],
                         (right, left)[sd])
            send(here, side_part(1, sd, SIDE[n]), mside_s.at[sd, n], mside_r.at[sd, n], mirror)

    def side_mirrored(which):
        for n in which:
            for sd in range(2):
                arrived(side_part(1, sd, SIDE[n]), mside_r.at[sd, n])

    first = blk * (4 * ROWS) + inner * ROWS

    def wanted(i, group):
        return [t_own[0, i, PER * group + b] for b in range(PER)]

    def parts(lhs, rhs):
        product = jnp.dot(lhs, rhs, preferred_element_type=jnp.float32)
        width = den.shape[3]
        return [product[:, b * width:(b + 1) * width] for b in range(PER)]

    def add(i, e, blocks, fresh=False):
        for b, block in enumerate(blocks):
            if fresh:
                out[i, PER * e + b] = block
            else:
                out[i, PER * e + b] += block

    def rights(rows, want):
        return right_side([
            [read(find(columns, column, places, empty)) for columns, places, empty, read in rows]
            for column in want
        ])

    def own_products(buffer, half, fresh):
        def body(i, carry):
            lhs = left_side([
                buffer[row, find([t_own[half, row, PER + a] for a in range(PER)],
                                 first + i, range(PER, 2 * PER), PER)]
                for row in range(ROWS)
            ])
            present = [
                find([t_own[half, row, PER + a] for a in range(PER)], first + i, (1, 1, 1), 0)
                for row in range(ROWS)
            ]
            for e in range(3):
                rows = [
                    ([jnp.where(present[row] == 1, t_own[half, row, PER * e + b], -1)
                      for b in range(PER)],
                     range(PER * e, PER * e + PER), NZ,
                     lambda s, row=row: buffer[row, s])
                    for row in range(ROWS)
                ]
                add(i, e, parts(lhs, rights(rows, wanted(i, e))), fresh)
            return carry
        lax.fori_loop(0, ROWS, body, 0)

    def lefts(names, reads, target):
        return left_side([read(find(name, target, range(PER), 0))
                          for name, read in zip(names, reads)])

    def guarded(name, columns, target):
        present = find(name, target, (1, 1, 1), 0) == 1
        return [jnp.where(present, column, -1) for column in columns]

    def entries(table, index, group):
        return [table[(*index, PER * group + b)] for b in range(PER)]

    two = [(half, sd) for half in range(2) for sd in range(2)]
    pair = [(half, row) for half in range(2) for row in range(ROWS)]

    def from_side(where, left_place, target, parts_wanted):
        buffers = (side0, side1, side2)
        names = [entries(t_side, index, theirs[left_place]) for index in where]

        def reader(place, index):
            return lambda s: buffers[place][(*index, s)]

        lhs = lefts(names, [reader(left_place, index) for index in where], target)
        for place, want in parts_wanted:
            rows = [(guarded(name, entries(t_side, index, theirs[place]), target),
                     range(PER), PER, reader(place, index))
                    for name, index in zip(names, where)]
            yield parts(lhs, rights(rows, want))

    def side_products(i):
        places = ((2, 1), (1, 2 - 2 * parity))
        for row in range(ROWS):
            blocks = from_side([(h, sd, row) for h, sd in two], 2, first + i,
                               [(place, wanted(i, e)) for place, e in places])
            for (_, e), block in zip(places, blocks):
                add(i, e, block)

    def first_of(device):
        return device[0] * (4 * ROWS) + device[1] * ROWS

    def x_partial(direction):
        device = (right, left)[direction]
        want = entries(t_side, (0, 1 - direction, direction), theirs[2])
        where = [(h, direction, row) for h, row in pair]
        (blocks,) = from_side(where, 1, first_of(device) + direction, [(2, want)])
        for b, block in enumerate(blocks):
            x_out[direction, b] = block

    def z_partial(i):
        want = [t_next[i, PER * 2 * parity + b] for b in range(PER)]
        sums = None
        for row in range(ROWS):
            (blocks,) = from_side([(h, sd, row) for h, sd in two], 0,
                                  first_of(z_to) + i, [(1, want)])
            sums = blocks if sums is None else [a + b for a, b in zip(sums, blocks)]
        for b, block in enumerate(sums):
            z_out[i, b] = block

    z_group = 2 - 2 * parity

    def za_products(i):
        for row in range(ROWS):
            names = [entries(t_z, (h, sd, row), z_group) for h, sd in two]
            reads = [lambda s, h=h, sd=sd: za[h, sd, row, s] for h, sd in two]
            rows = [(guarded(name, name, first + i), range(PER), PER, read)
                    for name, read in zip(names, reads)]
            add(i, 1, parts(lefts(names, reads, first + i), rights(rows, wanted(i, 1))))

    def far_lefts(i):
        names = [entries(t_far, (h, row), 1) for h, row in pair]
        reads = [lambda s, h=h, row=row: fb[h, row, s] for h, row in pair]
        lf[i] = lefts(names, reads, first + i)

    def far_products(g, i):
        buffer, group = (fa, fb)[g], mine[g]
        rows = [(guarded(entries(t_far, (h, row), 1), entries(t_far, (h, row), group), first + i),
                 range(PER), PER, lambda s, h=h, row=row: buffer[h, row, s])
                for h, row in pair]
        add(i, group, parts(lf[i], rights(rows, wanted(i, group))))

    def each_row(*steps):
        def body(i, carry):
            for step in steps:
                step(i)
            return carry
        lax.fori_loop(0, ROWS, body, 0)

    for copy in owned:
        copy.wait()
    tables[0].wait()
    own_products(own0, 0, True)

    for sd in range(2):
        arrived(c_side.at[0, sd], cs_r.at[sd])
        send(c_side.at[0, sd], c_z.at[0, sd], cz_s.at[sd], cz_r.at[sd], z_to)
        send(c_side.at[0, sd], c_side.at[1, sd], mc_s.at[1 + sd], mc_r.at[1 + sd], mirror)
    side_arrived(0)
    side_arrived(1)
    arrived(c_own, mc_r.at[0])
    load_table(1, c_own, t_own.at[1])
    for row in range(ROWS):
        arrived(own1.at[row, pl.ds(0, NZ)], mown_r.at[row])
    tables[1].wait()
    own_products(own1, 1, False)
    side_arrived(2)
    arrived(c_far.at[0], cf_r.at[0])
    send(c_far.at[0], c_far.at[1], mc_s.at[3], mc_r.at[3], mirror)
    for sd in range(2):
        arrived(c_z.at[0, sd], cz_r.at[sd])
        send(c_z.at[0, sd], c_z.at[1, sd], mc_s.at[4 + sd], mc_r.at[4 + sd], mirror)
    arrived(c_next, cn_r.at[0])
    z_arrived(0)
    z_arrived(1)
    for sd in range(2):
        arrived(c_side.at[1, sd], mc_r.at[1 + sd])
        arrived(c_z.at[1, sd], mc_r.at[4 + sd])
    arrived(c_far.at[1], mc_r.at[3])
    load_table(2, c_side, t_side)
    load_table(3, c_z, t_z)
    load_table(4, c_far, t_far)
    load_table(5, c_next, t_next)
    side_arrived(3)
    z_arrived(2)
    z_arrived(3)
    side_arrived(4)
    for k in (2, 3, 4, 5):
        tables[k].wait()
    side_mirrored(range(5))
    each_row(z_partial)
    z_arrived(4)
    z_arrived(5)
    for i in range(ROWS):
        send(z_out.at[i], z_in.at[i], zp_s.at[i], zp_r.at[i], z_to)
    side_arrived(5)
    for m in range(6):
        z_mirrored(m)
    each_row(za_products)
    side_arrived(6)
    side_mirrored((5, 6))
    for direction in range(2):
        x_partial(direction)
    far_arrived(0)
    for direction, device in enumerate((right, left)):
        send(x_out.at[direction], x_in.at[direction],
             xp_s.at[direction], xp_r.at[direction], device)
    each_row(side_products)
    far_arrived(1)
    for i in range(ROWS):
        arrived(z_in.at[i], zp_r.at[i])
        add(i, 2 * parity, [z_in[i, b] for b in range(PER)])
    far_mirrored(0)
    far_mirrored(1)
    each_row(far_lefts, lambda i: far_products(0, i), lambda i: far_products(1, i))
    for i in range(ROWS):
        arrived(x_in.at[i], xp_r.at[i])
        add(i, mine[2], [x_in[i, b] for b in range(PER)])
    for copy in sent:
        copy.wait_send()


def square_rows(density, block_cols):
    rows, nz, b, _ = density.shape
    f32, i32 = density.dtype, jnp.int32
    dma = pltpu.SemaphoreType.DMA
    anywhere = pl.BlockSpec(memory_space=pl.ANY)
    vmem, smem = pltpu.VMEM, pltpu.SMEM
    tables = [(rows, nz), (2, 2, rows, nz), (2, 2, rows, nz), (2, rows, nz)]
    return pl.pallas_call(
        square_kernel,
        out_shape=jax.ShapeDtypeStruct(density.shape, f32),
        in_specs=[anywhere, anywhere],
        out_specs=pl.BlockSpec(memory_space=pltpu.VMEM),
        scratch_shapes=[
            vmem((rows, nz + 1, b, b), f32), vmem((rows, nz + 1, b, b), f32),
            *[vmem((2, 2, rows, PER + 1, b, b), f32)] * 4,
            *[vmem((2, rows, PER + 1, b, b), f32)] * 2,
            *[vmem((2, PER, b, b), f32)] * 4,
            vmem((rows, b, 12 * b), jnp.bfloat16),
            *[vmem(shape, i32) for shape in tables], vmem((rows, nz), i32),
            smem((2, rows, nz), i32), *[smem(shape, i32) for shape in tables[1:]],
            smem((rows, nz), i32),
            dma((2, 7)), dma((2, 7)), dma((2, 3)), dma((2, 3)), dma((6,)), dma((6,)),
            dma((2,)), dma((2,)), dma((2, 3)), dma((2, 3)),
            dma((2, 7)), dma((2, 7)), dma((6,)), dma((6,)),
            dma((2,)), dma((2,)), dma((2,)), dma((2,)), dma((1,)), dma((1,)),
            dma((1,)), dma((1,)), dma((6,)), dma((6,)),
            dma((2,)), dma((2,)), dma((2,)), dma((2,)), dma((2,)), dma((6,)),
        ],
        compiler_params=pltpu.CompilerParams(
            collective_id=0, has_side_effects=True, vmem_limit_bytes=24 * 2**20),
    )(pltpu.with_memory_space_constraint(density, pltpu.HBM),
      pltpu.with_memory_space_constraint(block_cols, pltpu.HBM))


def shards(density, block_cols, targets):
    del targets
    return 2.0 * density - square_rows(density, block_cols)


def solution(mesh):
    return jax.shard_map(
        shards,
        mesh=mesh,
        in_specs=(
            P(("blk", "inner"), None, None, None),
            P(("blk", "inner"), None),
            P(("blk", "inner"), None, None),
        ),
        out_specs=P(("blk", "inner"), None, None, None),
        check_vma=False,
    )
```

```python
import jax
import jax.numpy as jnp
from jax import lax
from jax.experimental import pallas as pl
from jax.experimental.pallas import tpu as pltpu
from jax.sharding import PartitionSpec as P

MESH = pl.DeviceIdType.MESH
PER = 3
NZ = 9
X = 4
ROWS = 2


def split(value):
    high = value.astype(jnp.bfloat16)
    return high, (value - high.astype(jnp.float32)).astype(jnp.bfloat16)


def find(columns, wanted, places, otherwise):
    place = jnp.int32(otherwise)
    for column, here in zip(columns, places):
        place = jnp.where(column == wanted, here, place)
    return place


def left_side(blocks):
    highs, lows = zip(*(split(block.T) for block in blocks))
    return jnp.concatenate(highs + lows + highs, axis=1)


def right_side(columns_of_blocks):
    columns = []
    for blocks in columns_of_blocks:
        highs, lows = zip(*(split(block) for block in blocks))
        columns.append(jnp.concatenate(highs + highs + lows, axis=0))
    return jnp.concatenate(columns, axis=1)


def square_kernel(
    den, cols, out,
    own0, own1, p1, p2, q0, q1, d0, d1, f0, f1, p_out, p_in, q_out, q_in,
    c_own, c_p, c_q, c_d, c_f, t_own, t_p, t_q, t_d, t_f,
    send_s, recv_s, mirror_s, mirrored_s, own_s, own_r, table_send, table_recv,
    table_out, table_back, part_s, part_r, local_s, table_s,
):
    blk = lax.axis_index("blk")
    inner = lax.axis_index("inner")
    strips = lax.axis_size("blk")
    parity = lax.rem(blk, 2)
    core = lax.rem(inner, 2)
    chip_x = 2 * (inner // 2) + parity

    def at_x(x):
        x = lax.rem(x, X)
        return (blk - parity + lax.rem(x, 2), 2 * (x // 2) + core)

    p_chip = at_x(chip_x + 1 + 2 * parity)
    q_chip = at_x(chip_x + 3 - 2 * parity)
    mirror = (blk, inner + 1 - 2 * core)
    f_to = (lax.rem(blk + strips + 2 - 4 * parity, strips), inner)
    d_to = (lax.rem(blk + strips - 2 + 4 * parity, strips), inner)

    barrier = pltpu.get_barrier_semaphore()
    for device in (p_chip, q_chip, mirror, f_to, d_to):
        pl.semaphore_signal(barrier, inc=1, device_id=device, device_id_type=MESH)

    owned = []
    for row in range(ROWS):
        copy = pltpu.make_async_copy(den.at[row], own0.at[row, pl.ds(0, NZ)], local_s.at[row])
        copy.start()
        owned.append(copy)
    tables = [pltpu.make_async_copy(cols, t_own.at[0], table_s.at[0])]
    tables[0].start()

    none = jnp.zeros(den.shape[2:], jnp.float32)
    for row in range(ROWS):
        own0[row, NZ] = none
        own1[row, NZ] = none
        for half in range(2):
            for buffer in (p1, p2, q0, q1, d0, d1, f0, f1):
                buffer[half, row, PER] = none

    pl.semaphore_wait(barrier, 5)

    sent = []

    def send(src, dst, s, r, device):
        copy = pltpu.make_async_remote_copy(
            src_ref=src, dst_ref=dst, send_sem=s, recv_sem=r,
            device_id=device, device_id_type=MESH,
        )
        copy.start()
        sent.append(copy)

    def arrived(dst, r):
        pltpu.make_async_remote_copy(
            src_ref=dst, dst_ref=dst, send_sem=r, recv_sem=r,
            device_id=mirror, device_id_type=MESH,
        ).wait_recv()

    def groups(p):
        return (2 * p, 1, 2 - 2 * p)

    def slots(group):
        return pl.ds(PER * group, PER)

    mine = groups(parity)
    theirs = groups(1 - parity)

    P_FLOW, Q_FLOW, D_FLOW, F_FLOW = range(4)
    buffers = {P_FLOW: {1: p1, 2: p2}, Q_FLOW: {1: q1, 0: q0},
               D_FLOW: {0: d0, 1: d1}, F_FLOW: {1: f1, 0: f0}}
    order = {P_FLOW: (1, 2), Q_FLOW: (1, 0), D_FLOW: (0, 1), F_FLOW: (1, 0)}
    c_table = (c_p, c_q, c_d, c_f)
    t_table = (t_p, t_q, t_d, t_f)

    def piece(flow, half, g, row):
        return buffers[flow][g].at[half, row, pl.ds(0, PER)]

    def place(flow, g, row):
        return 2 * order[flow].index(g) + row

    for flow, device in ((P_FLOW, p_chip), (Q_FLOW, q_chip), (D_FLOW, d_to)):
        send(cols, c_table[flow].at[0], table_send.at[flow], table_recv.at[flow], device)
    for step in range(2):
        for row in range(ROWS):
            for flow, device in ((Q_FLOW, q_chip), (P_FLOW, p_chip), (D_FLOW, d_to)):
                g = order[flow][step]
                n = place(flow, g, row)
                send(den.at[row, slots(mine[g])], piece(flow, 0, g, row),
                     send_s.at[flow, n], recv_s.at[flow, n], device)
    send(cols, c_own, own_s.at[ROWS], own_r.at[ROWS], mirror)
    for row in range(ROWS):
        send(den.at[row], own1.at[row, pl.ds(0, NZ)], own_s.at[row], own_r.at[row], mirror)

    def load_table(k, src, dst):
        copy = pltpu.make_async_copy(src, dst, table_s.at[k])
        copy.start()
        tables.append(copy)

    def flow_arrived(flow, step, row):
        g = order[flow][step]
        n = place(flow, g, row)
        arrived(piece(flow, 0, g, row), recv_s.at[flow, n])
        if flow == Q_FLOW:
            m = place(F_FLOW, g, row)
            send(piece(flow, 0, g, row), piece(F_FLOW, 0, g, row),
                 send_s.at[F_FLOW, m], recv_s.at[F_FLOW, m], f_to)
        send(piece(flow, 0, g, row), piece(flow, 1, g, row),
             mirror_s.at[flow, n], mirrored_s.at[flow, n], mirror)

    def mirrored(flow, g):
        for row in range(ROWS):
            arrived(piece(flow, 1, g, row), mirrored_s.at[flow, place(flow, g, row)])

    def table_arrived(flow):
        arrived(c_table[flow].at[0], table_recv.at[flow])
        if flow == Q_FLOW:
            send(c_q.at[0], c_f.at[0], table_send.at[F_FLOW], table_recv.at[F_FLOW], f_to)
        send(c_table[flow].at[0], c_table[flow].at[1], table_out.at[flow],
             table_back.at[flow], mirror)

    def first_of(device):
        return device[0] * (4 * ROWS) + device[1] * ROWS

    first, p_first, q_first = first_of((blk, inner)), first_of(p_chip), first_of(q_chip)

    def parts(lhs, rhs):
        product = jnp.dot(lhs, rhs, preferred_element_type=jnp.float32)
        width = den.shape[3]
        return [product[:, b * width:(b + 1) * width] for b in range(PER)]

    def entries(table, index, group):
        return [table[(*index, PER * group + b)] for b in range(PER)]

    def add(i, group, blocks, fresh=False):
        for b, block in enumerate(blocks):
            if fresh:
                out[i, PER * group + b] = block
            else:
                out[i, PER * group + b] += block

    pair = [(half, row) for half in range(2) for row in range(ROWS)]

    def products(target, left, wanted):
        names, reads = left
        lhs = left_side([read(find(name, target, range(PER), 0))
                         for name, read in zip(names, reads)])
        present = [find(name, target, (1, 1, 1), 0) == 1 for name in names]
        for (columns, blocks), want in wanted:
            columns = [[jnp.where(there, c, -1) for c in row]
                       for there, row in zip(present, columns)]
            rhs = right_side([
                [read(find(row, column, range(PER), empty))
                 for row, (read, empty) in zip(columns, blocks)]
                for column in want
            ])
            yield parts(lhs, rhs)

    def of_flow(flow, g, parity_there):
        buffer = buffers[flow][g]
        names = [entries(t_table[flow], index, groups(parity_there)[g]) for index in pair]
        reads = [lambda s, index=index: buffer[(*index, s)] for index in pair]
        return names, reads

    def right_of_flow(flow, g, parity_there):
        names, reads = of_flow(flow, g, parity_there)
        return names, [(read, PER) for read in reads]

    def of_own(group):
        names = [entries(t_own, index, group) for index in pair]
        reads = [lambda s, buffer=(own0, own1)[half], row=row: buffer[row, PER * group + s]
                 for half, row in pair]
        return names, reads

    def right_of_own(group):
        names, reads = of_own(group)
        return names, [(read, NZ - PER * group) for read in reads]

    def want(i, group):
        return entries(t_own, (0, i), group)

    def own_products(i):
        for e, blocks in enumerate(products(
                first + i, of_own(1), [(right_of_own(e), want(i, e)) for e in range(3)])):
            add(i, e, blocks, fresh=True)

    def store(ref, k, i, blocks, fresh=False):
        for b, block in enumerate(blocks):
            if fresh:
                ref[k, i, b] = block
            else:
                ref[k, i, b] += block

    def q_own(i):
        wanted = [(right_of_own(mine[2]), entries(t_q, (0, i), 1)),
                  (right_of_own(1), entries(t_q, (0, i), theirs[2]))]
        for k, blocks in enumerate(products(q_first + i, of_own(mine[2]), wanted)):
            store(q_out, k, i, blocks, fresh=True)

    def q_part(k, i):
        g = (1, 2)[k]
        (blocks,) = products(q_first + i, of_flow(P_FLOW, 1, 1 - parity), [
            (right_of_flow(P_FLOW, g, 1 - parity), entries(t_q, (0, i), theirs[g]))])
        store(q_out, k, i, blocks)

    def p_part(k, i):
        g = (0, 1)[k]
        (blocks,) = products(p_first + i, of_flow(D_FLOW, 0, parity), [
            (right_of_flow(D_FLOW, g, parity), entries(t_p, (0, i), theirs[(1, 0)[k]]))])
        store(p_out, k, i, blocks, fresh=True)

    def p_part_q(i):
        (blocks,) = products(p_first + i, of_flow(Q_FLOW, 1, 1 - parity), [
            (right_of_flow(Q_FLOW, 0, 1 - parity), entries(t_p, (0, i), theirs[0]))])
        store(p_out, 1, i, blocks)

    def from_p(i):
        wanted = [(right_of_flow(P_FLOW, 2, 1 - parity), want(i, 1)),
                  (right_of_flow(P_FLOW, 1, 1 - parity), want(i, mine[2]))]
        for group, blocks in zip((1, mine[2]), products(
                first + i, of_flow(P_FLOW, 2, 1 - parity), wanted)):
            add(i, group, blocks)

    def from_f(i):
        wanted = [(right_of_flow(F_FLOW, 0, 1 - parity), want(i, 1)),
                  (right_of_flow(F_FLOW, 1, 1 - parity), want(i, mine[0]))]
        for group, blocks in zip((1, mine[0]), products(
                first + i, of_flow(F_FLOW, 0, 1 - parity), wanted)):
            add(i, group, blocks)

    def each_row(*steps):
        def body(i, carry):
            for step in steps:
                step(i)
            return carry
        lax.fori_loop(0, ROWS, body, 0)

    def send_part(k, i):
        for n, (src, dst, device) in enumerate(((q_out, q_in, q_chip), (p_out, p_in, p_chip))):
            send(src.at[k, i], dst.at[k, i], part_s.at[n, 2 * k + i], part_r.at[n, 2 * k + i],
                 device)

    def part_arrived(k, i):
        for n, (ref, group) in enumerate(((q_in, (1, mine[2])[k]), (p_in, (1, mine[0])[k]))):
            arrived(ref.at[k, i], part_r.at[n, 2 * k + i])
            add(i, group, [ref[k, i, b] for b in range(PER)])

    raw = (Q_FLOW, P_FLOW, D_FLOW)
    for flow in raw:
        table_arrived(flow)
    arrived(c_own, own_r.at[ROWS])
    load_table(1, c_own, t_own.at[1])
    for copy in owned:
        copy.wait()
    for row in range(ROWS):
        arrived(own1.at[row, pl.ds(0, NZ)], own_r.at[row])
    for k in range(2):
        tables[k].wait()
    each_row(own_products)
    table_arrived(F_FLOW)
    for flow in raw:
        flow_arrived(flow, 0, 0)
    for flow in (*raw, F_FLOW):
        arrived(c_table[flow].at[1], table_back.at[flow])
        load_table(2 + flow, c_table[flow], t_table[flow])
    for k in range(2, 6):
        tables[k].wait()
    each_row(q_own)
    for flow in raw:
        flow_arrived(flow, 0, 1)
    flow_arrived(F_FLOW, 0, 0)
    mirrored(P_FLOW, 1)
    mirrored(D_FLOW, 0)
    mirrored(Q_FLOW, 1)
    each_row(lambda i: q_part(0, i), lambda i: p_part(0, i))
    for flow in raw:
        flow_arrived(flow, 1, 0)
    for i in range(ROWS):
        send_part(0, i)
    flow_arrived(F_FLOW, 0, 1)
    for flow in raw:
        flow_arrived(flow, 1, 1)
    mirrored(P_FLOW, 2)
    mirrored(D_FLOW, 1)
    mirrored(Q_FLOW, 0)
    for i in range(ROWS):
        q_part(1, i)
        p_part(1, i)
        p_part_q(i)
        send_part(1, i)
    flow_arrived(F_FLOW, 1, 0)
    flow_arrived(F_FLOW, 1, 1)
    each_row(from_p)
    mirrored(F_FLOW, 1)
    mirrored(F_FLOW, 0)
    each_row(from_f)
    for k in range(2):
        for i in range(ROWS):
            part_arrived(k, i)
    for copy in sent:
        copy.wait_send()


def square_rows(density, block_cols):
    rows, nz, b, _ = density.shape
    f32, i32 = density.dtype, jnp.int32
    dma = pltpu.SemaphoreType.DMA
    anywhere = pl.BlockSpec(memory_space=pl.ANY)
    vmem, smem = pltpu.VMEM, pltpu.SMEM
    return pl.pallas_call(
        square_kernel,
        out_shape=jax.ShapeDtypeStruct(density.shape, f32),
        in_specs=[anywhere, anywhere],
        out_specs=pl.BlockSpec(memory_space=pltpu.VMEM),
        scratch_shapes=[
            *[vmem((rows, nz + 1, b, b), f32)] * 2,
            *[vmem((2, rows, PER + 1, b, b), f32)] * 8,
            *[vmem((2, rows, PER, b, b), f32)] * 4,
            vmem((rows, nz), i32), *[vmem((2, rows, nz), i32)] * 4,
            *[smem((2, rows, nz), i32)] * 5,
            dma((4, 4)), dma((4, 4)), dma((4, 4)), dma((4, 4)),
            dma((3,)), dma((3,)), dma((4,)), dma((4,)), dma((4,)), dma((4,)),
            dma((2, 4)), dma((2, 4)), dma((2,)), dma((6,)),
        ],
        compiler_params=pltpu.CompilerParams(
            collective_id=0, has_side_effects=True, vmem_limit_bytes=24 * 2**20),
    )(pltpu.with_memory_space_constraint(density, pltpu.HBM),
      pltpu.with_memory_space_constraint(block_cols, pltpu.HBM))


def shards(density, block_cols, targets):
    del targets
    return 2.0 * density - square_rows(density, block_cols)


def solution(mesh):
    return jax.shard_map(
        shards,
        mesh=mesh,
        in_specs=(
            P(("blk", "inner"), None, None, None),
            P(("blk", "inner"), None),
            P(("blk", "inner"), None, None),
        ),
        out_specs=P(("blk", "inner"), None, None, None),
        check_vma=False,
    )
```

```python
import jax
import jax.numpy as jnp
from jax import lax
from jax.experimental import pallas as pl
from jax.experimental.pallas import tpu as pltpu
from jax.sharding import PartitionSpec as P

MESH = pl.DeviceIdType.MESH
PER = 3
NZ = 9
X = 4
ROWS = 2


def split(value):
    high = value.astype(jnp.bfloat16)
    return high, (value - high.astype(jnp.float32)).astype(jnp.bfloat16)


def find(columns, wanted, places, otherwise):
    place = jnp.int32(otherwise)
    for column, here in zip(columns, places):
        place = jnp.where(column == wanted, here, place)
    return place


def left_side(blocks):
    highs, lows = zip(*(split(block.T) for block in blocks))
    return jnp.concatenate(highs + lows + highs, axis=1)


def right_side(columns_of_blocks):
    columns = []
    for blocks in columns_of_blocks:
        highs, lows = zip(*(split(block) for block in blocks))
        columns.append(jnp.concatenate(highs + highs + lows, axis=0))
    return jnp.concatenate(columns, axis=1)


def square_kernel(
    den, cols, out,
    own0, own1, p1, p2, q0, q1, d0, d1, f0, f1, p_out, p_in, q_out, q_in,
    c_own, c_p, c_q, c_d, c_f, t_own, t_p, t_q, t_d, t_f,
    send_s, recv_s, mirror_s, mirrored_s, own_s, own_r, table_send, table_recv,
    table_out, table_back, part_s, part_r, local_s, table_s,
):
    blk = lax.axis_index("blk")
    inner = lax.axis_index("inner")
    strips = lax.axis_size("blk")
    parity = lax.rem(blk, 2)
    core = lax.rem(inner, 2)
    chip_x = 2 * (inner // 2) + parity

    def at_x(x):
        x = lax.rem(x, X)
        return (blk - parity + lax.rem(x, 2), 2 * (x // 2) + core)

    p_chip = at_x(chip_x + 1 + 2 * parity)
    q_chip = at_x(chip_x + 3 - 2 * parity)
    mirror = (blk, inner + 1 - 2 * core)
    f_to = (lax.rem(blk + strips + 2 - 4 * parity, strips), inner)
    d_to = (lax.rem(blk + strips - 2 + 4 * parity, strips), inner)

    barrier = pltpu.get_barrier_semaphore()
    for device in (p_chip, q_chip, mirror):
        pl.semaphore_signal(barrier, inc=1, device_id=device, device_id_type=MESH)

    owned = []
    for row in range(ROWS):
        copy = pltpu.make_async_copy(den.at[row], own0.at[row, pl.ds(0, NZ)], local_s.at[row])
        copy.start()
        owned.append(copy)
    tables = [pltpu.make_async_copy(cols, t_own.at[0], table_s.at[0])]
    tables[0].start()

    none = jnp.zeros(den.shape[2:], jnp.float32)
    for row in range(ROWS):
        own0[row, NZ] = none
        own1[row, NZ] = none
        for half in range(2):
            for buffer in (p1, p2, q0, q1, d0, d1, f0, f1):
                buffer[half, row, PER] = none

    even_z = lax.rem(blk // 2, 2) == 0

    @pl.when(even_z)
    def _():
        pl.semaphore_wait(barrier, 3)

    @pl.when(jnp.logical_not(even_z))
    def _():
        pl.semaphore_wait(barrier, 5)

    for device in (f_to, d_to):
        pl.semaphore_signal(barrier, inc=1, device_id=device, device_id_type=MESH)

    sent = []

    def send(src, dst, s, r, device):
        copy = pltpu.make_async_remote_copy(
            src_ref=src, dst_ref=dst, send_sem=s, recv_sem=r,
            device_id=device, device_id_type=MESH,
        )
        copy.start()
        sent.append(copy)

    def arrived(dst, r):
        pltpu.make_async_remote_copy(
            src_ref=dst, dst_ref=dst, send_sem=r, recv_sem=r,
            device_id=mirror, device_id_type=MESH,
        ).wait_recv()

    def groups(p):
        return (2 * p, 1, 2 - 2 * p)

    def slots(group):
        return pl.ds(PER * group, PER)

    mine = groups(parity)
    theirs = groups(1 - parity)

    P_FLOW, Q_FLOW, D_FLOW, F_FLOW = range(4)
    buffers = {P_FLOW: {1: p1, 2: p2}, Q_FLOW: {1: q1, 0: q0},
               D_FLOW: {0: d0, 1: d1}, F_FLOW: {1: f1, 0: f0}}
    order = {P_FLOW: (1, 2), Q_FLOW: (1, 0), D_FLOW: (0, 1), F_FLOW: (1, 0)}
    c_table = (c_p, c_q, c_d, c_f)
    t_table = (t_p, t_q, t_d, t_f)

    def piece(flow, half, g, row):
        return buffers[flow][g].at[half, row, pl.ds(0, PER)]

    def place(flow, g, row):
        return 2 * order[flow].index(g) + row

    def send_flows(*flows):
        for flow, device in flows:
            send(cols, c_table[flow].at[0], table_send.at[flow], table_recv.at[flow], device)
        for step in range(2):
            for row in range(ROWS):
                for flow, device in flows:
                    g = order[flow][step]
                    n = place(flow, g, row)
                    send(den.at[row, slots(mine[g])], piece(flow, 0, g, row),
                         send_s.at[flow, n], recv_s.at[flow, n], device)

    send_flows((Q_FLOW, q_chip), (P_FLOW, p_chip))
    send(cols, c_own, own_s.at[ROWS], own_r.at[ROWS], mirror)
    for row in range(ROWS):
        send(den.at[row], own1.at[row, pl.ds(0, NZ)], own_s.at[row], own_r.at[row], mirror)

    @pl.when(even_z)
    def _():
        pl.semaphore_wait(barrier, 2)

    send_flows((D_FLOW, d_to))

    def load_table(k, src, dst):
        copy = pltpu.make_async_copy(src, dst, table_s.at[k])
        copy.start()
        tables.append(copy)

    def flow_arrived(flow, step, row):
        g = order[flow][step]
        n = place(flow, g, row)
        arrived(piece(flow, 0, g, row), recv_s.at[flow, n])
        if flow == Q_FLOW:
            m = place(F_FLOW, g, row)
            send(piece(flow, 0, g, row), piece(F_FLOW, 0, g, row),
                 send_s.at[F_FLOW, m], recv_s.at[F_FLOW, m], f_to)
        send(piece(flow, 0, g, row), piece(flow, 1, g, row),
             mirror_s.at[flow, n], mirrored_s.at[flow, n], mirror)

    def mirrored(flow, g):
        for row in range(ROWS):
            arrived(piece(flow, 1, g, row), mirrored_s.at[flow, place(flow, g, row)])

    def table_arrived(flow):
        arrived(c_table[flow].at[0], table_recv.at[flow])
        if flow == Q_FLOW:
            send(c_q.at[0], c_f.at[0], table_send.at[F_FLOW], table_recv.at[F_FLOW], f_to)
        send(c_table[flow].at[0], c_table[flow].at[1], table_out.at[flow],
             table_back.at[flow], mirror)

    def first_of(device):
        return device[0] * (4 * ROWS) + device[1] * ROWS

    first, p_first, q_first = first_of((blk, inner)), first_of(p_chip), first_of(q_chip)

    def parts(lhs, rhs):
        product = jnp.dot(lhs, rhs, preferred_element_type=jnp.float32)
        width = den.shape[3]
        return [product[:, b * width:(b + 1) * width] for b in range(PER)]

    def entries(table, index, group):
        return [table[(*index, PER * group + b)] for b in range(PER)]

    def add(i, group, blocks, fresh=False):
        for b, block in enumerate(blocks):
            if fresh:
                out[i, PER * group + b] = block
            else:
                out[i, PER * group + b] += block

    pair = [(half, row) for half in range(2) for row in range(ROWS)]

    def products(target, left, wanted):
        names, reads = left
        lhs = left_side([read(find(name, target, range(PER), 0))
                         for name, read in zip(names, reads)])
        present = [find(name, target, (1, 1, 1), 0) == 1 for name in names]
        for (columns, blocks), want in wanted:
            columns = [[jnp.where(there, c, -1) for c in row]
                       for there, row in zip(present, columns)]
            rhs = right_side([
                [read(find(row, column, range(PER), empty))
                 for row, (read, empty) in zip(columns, blocks)]
                for column in want
            ])
            yield parts(lhs, rhs)

    def of_flow(flow, g, parity_there):
        buffer = buffers[flow][g]
        names = [entries(t_table[flow], index, groups(parity_there)[g]) for index in pair]
        reads = [lambda s, index=index: buffer[(*index, s)] for index in pair]
        return names, reads

    def right_of_flow(flow, g, parity_there):
        names, reads = of_flow(flow, g, parity_there)
        return names, [(read, PER) for read in reads]

    def of_own(group):
        names = [entries(t_own, index, group) for index in pair]
        reads = [lambda s, buffer=(own0, own1)[half], row=row: buffer[row, PER * group + s]
                 for half, row in pair]
        return names, reads

    def right_of_own(group):
        names, reads = of_own(group)
        return names, [(read, NZ - PER * group) for read in reads]

    def want(i, group):
        return entries(t_own, (0, i), group)

    def own_products(i):
        for e, blocks in enumerate(products(
                first + i, of_own(1), [(right_of_own(e), want(i, e)) for e in range(3)])):
            add(i, e, blocks, fresh=True)

    def store(ref, k, i, blocks, fresh=False):
        for b, block in enumerate(blocks):
            if fresh:
                ref[k, i, b] = block
            else:
                ref[k, i, b] += block

    def q_own(i):
        wanted = [(right_of_own(mine[2]), entries(t_q, (0, i), 1)),
                  (right_of_own(1), entries(t_q, (0, i), theirs[2]))]
        for k, blocks in enumerate(products(q_first + i, of_own(mine[2]), wanted)):
            store(q_out, k, i, blocks, fresh=True)

    def q_part(k, i):
        g = (1, 2)[k]
        (blocks,) = products(q_first + i, of_flow(P_FLOW, 1, 1 - parity), [
            (right_of_flow(P_FLOW, g, 1 - parity), entries(t_q, (0, i), theirs[g]))])
        store(q_out, k, i, blocks)

    def p_part(k, i):
        g = (0, 1)[k]
        (blocks,) = products(p_first + i, of_flow(D_FLOW, 0, parity), [
            (right_of_flow(D_FLOW, g, parity), entries(t_p, (0, i), theirs[(1, 0)[k]]))])
        store(p_out, k, i, blocks, fresh=True)

    def p_part_q(i):
        (blocks,) = products(p_first + i, of_flow(Q_FLOW, 1, 1 - parity), [
            (right_of_flow(Q_FLOW, 0, 1 - parity), entries(t_p, (0, i), theirs[0]))])
        store(p_out, 1, i, blocks)

    def from_p(i):
        wanted = [(right_of_flow(P_FLOW, 2, 1 - parity), want(i, 1)),
                  (right_of_flow(P_FLOW, 1, 1 - parity), want(i, mine[2]))]
        for group, blocks in zip((1, mine[2]), products(
                first + i, of_flow(P_FLOW, 2, 1 - parity), wanted)):
            add(i, group, blocks)

    def from_f(i):
        wanted = [(right_of_flow(F_FLOW, 0, 1 - parity), want(i, 1)),
                  (right_of_flow(F_FLOW, 1, 1 - parity), want(i, mine[0]))]
        for group, blocks in zip((1, mine[0]), products(
                first + i, of_flow(F_FLOW, 0, 1 - parity), wanted)):
            add(i, group, blocks)

    def each_row(*steps):
        def body(i, carry):
            for step in steps:
                step(i)
            return carry
        lax.fori_loop(0, ROWS, body, 0)

    def send_part(k, i):
        for n, (src, dst, device) in enumerate(((q_out, q_in, q_chip), (p_out, p_in, p_chip))):
            send(src.at[k, i], dst.at[k, i], part_s.at[n, 2 * k + i], part_r.at[n, 2 * k + i],
                 device)

    def part_arrived(k, i):
        for n, (ref, group) in enumerate(((q_in, (1, mine[2])[k]), (p_in, (1, mine[0])[k]))):
            arrived(ref.at[k, i], part_r.at[n, 2 * k + i])
            add(i, group, [ref[k, i, b] for b in range(PER)])

    raw = (Q_FLOW, P_FLOW, D_FLOW)
    for flow in raw:
        table_arrived(flow)
    arrived(c_own, own_r.at[ROWS])
    load_table(1, c_own, t_own.at[1])
    for copy in owned:
        copy.wait()
    for row in range(ROWS):
        arrived(own1.at[row, pl.ds(0, NZ)], own_r.at[row])
    for k in range(2):
        tables[k].wait()
    each_row(own_products)
    table_arrived(F_FLOW)
    for flow in raw:
        flow_arrived(flow, 0, 0)
    for flow in (*raw, F_FLOW):
        arrived(c_table[flow].at[1], table_back.at[flow])
        load_table(2 + flow, c_table[flow], t_table[flow])
    for k in range(2, 6):
        tables[k].wait()
    each_row(q_own)
    for flow in raw:
        flow_arrived(flow, 0, 1)
    flow_arrived(F_FLOW, 0, 0)
    mirrored(P_FLOW, 1)
    mirrored(D_FLOW, 0)
    mirrored(Q_FLOW, 1)
    each_row(lambda i: q_part(0, i), lambda i: p_part(0, i))
    for flow in raw:
        flow_arrived(flow, 1, 0)
    for i in range(ROWS):
        send_part(0, i)
    flow_arrived(F_FLOW, 0, 1)
    for flow in raw:
        flow_arrived(flow, 1, 1)
    mirrored(P_FLOW, 2)
    mirrored(D_FLOW, 1)
    mirrored(Q_FLOW, 0)
    for i in range(ROWS):
        q_part(1, i)
        p_part(1, i)
        p_part_q(i)
        send_part(1, i)
    flow_arrived(F_FLOW, 1, 0)
    flow_arrived(F_FLOW, 1, 1)
    each_row(from_p)
    mirrored(F_FLOW, 1)
    mirrored(F_FLOW, 0)
    each_row(from_f)
    for k in range(2):
        for i in range(ROWS):
            part_arrived(k, i)
    for copy in sent:
        copy.wait_send()


def square_rows(density, block_cols):
    rows, nz, b, _ = density.shape
    f32, i32 = density.dtype, jnp.int32
    dma = pltpu.SemaphoreType.DMA
    anywhere = pl.BlockSpec(memory_space=pl.ANY)
    vmem, smem = pltpu.VMEM, pltpu.SMEM
    return pl.pallas_call(
        square_kernel,
        out_shape=jax.ShapeDtypeStruct(density.shape, f32),
        in_specs=[anywhere, anywhere],
        out_specs=pl.BlockSpec(memory_space=pltpu.VMEM),
        scratch_shapes=[
            *[vmem((rows, nz + 1, b, b), f32)] * 2,
            *[vmem((2, rows, PER + 1, b, b), f32)] * 8,
            *[vmem((2, rows, PER, b, b), f32)] * 4,
            vmem((rows, nz), i32), *[vmem((2, rows, nz), i32)] * 4,
            *[smem((2, rows, nz), i32)] * 5,
            dma((4, 4)), dma((4, 4)), dma((4, 4)), dma((4, 4)),
            dma((3,)), dma((3,)), dma((4,)), dma((4,)), dma((4,)), dma((4,)),
            dma((2, 4)), dma((2, 4)), dma((2,)), dma((6,)),
        ],
        compiler_params=pltpu.CompilerParams(
            collective_id=0, has_side_effects=True, vmem_limit_bytes=24 * 2**20),
    )(pltpu.with_memory_space_constraint(density, pltpu.HBM),
      pltpu.with_memory_space_constraint(block_cols, pltpu.HBM))


def shards(density, block_cols, targets):
    del targets
    return 2.0 * density - square_rows(density, block_cols)


def solution(mesh):
    return jax.shard_map(
        shards,
        mesh=mesh,
        in_specs=(
            P(("blk", "inner"), None, None, None),
            P(("blk", "inner"), None),
            P(("blk", "inner"), None, None),
        ),
        out_specs=P(("blk", "inner"), None, None, None),
        check_vma=False,
    )
```

```python
import jax
import jax.numpy as jnp
from jax import lax
from jax.experimental import pallas as pl
from jax.experimental.pallas import tpu as pltpu
from jax.sharding import PartitionSpec as P

MESH = pl.DeviceIdType.MESH
PER = 3
NZ = 9
X = 4
Z = 8
ROWS = 2


def split(value):
    high = value.astype(jnp.bfloat16)
    return high, (value - high.astype(jnp.float32)).astype(jnp.bfloat16)


def find(columns, wanted, places, otherwise):
    place = jnp.int32(otherwise)
    for column, here in zip(columns, places):
        place = jnp.where(column == wanted, here, place)
    return place


def left_side(blocks):
    highs, lows = zip(*(split(block.T) for block in blocks))
    return jnp.concatenate(highs + lows + highs, axis=1)


def right_side(columns_of_blocks):
    columns = []
    for blocks in columns_of_blocks:
        highs, lows = zip(*(split(block) for block in blocks))
        columns.append(jnp.concatenate(highs + highs + lows, axis=0))
    return jnp.concatenate(columns, axis=1)


def purify_kernel(
    den, cols, out,
    own0, own1, p1, p2, q0, q1, d0, d1, f0, f1, p_out, p_in, q_out, q_in,
    c_own, c_p, c_q, c_d, c_f, t_own, t_p, t_q, t_d, t_f,
    send_s, recv_s, mirror_s, mirrored_s, own_s, own_r, table_send, table_recv,
    table_out, table_back, part_s, part_r, local_s, table_s,
):
    blk = lax.axis_index("blk")
    inner = lax.axis_index("inner")
    strips = lax.axis_size("blk")
    parity = lax.rem(blk, 2)
    core = lax.rem(inner, 2)
    chip_x = 2 * (inner // 2) + parity

    def at_x(x):
        x = lax.rem(x, X)
        return (blk - parity + lax.rem(x, 2), 2 * (x // 2) + core)

    p_chip = at_x(chip_x + 1 + 2 * parity)
    q_chip = at_x(chip_x + 3 - 2 * parity)
    mirror = (blk, inner + 1 - 2 * core)
    f_to = (lax.rem(blk + strips + 2 - 4 * parity, strips), inner)
    d_to = (lax.rem(blk + strips - 2 + 4 * parity, strips), inner)

    barrier = pltpu.get_barrier_semaphore()
    for device in (p_chip, q_chip, mirror):
        pl.semaphore_signal(barrier, inc=1, device_id=device, device_id_type=MESH)

    owned = []
    for row in range(ROWS):
        copy = pltpu.make_async_copy(den.at[row], own0.at[row, pl.ds(0, NZ)], local_s.at[row])
        copy.start()
        owned.append(copy)
    tables = [pltpu.make_async_copy(cols, t_own.at[0], table_s.at[0])]
    tables[0].start()

    none = jnp.zeros(den.shape[2:], jnp.float32)
    for row in range(ROWS):
        own0[row, NZ] = none
        own1[row, NZ] = none
        for half in range(2):
            for buffer in (p1, p2, q0, q1, d0, d1, f0, f1):
                buffer[half, row, PER] = none

    even_z = lax.rem(blk // 2, 2) == 0

    @pl.when(even_z)
    def _():
        pl.semaphore_wait(barrier, 3)

    @pl.when(jnp.logical_not(even_z))
    def _():
        pl.semaphore_wait(barrier, 5)

    for device in (f_to, d_to):
        pl.semaphore_signal(barrier, inc=1, device_id=device, device_id_type=MESH)

    sent = []

    def send(src, dst, s, r, device):
        copy = pltpu.make_async_remote_copy(
            src_ref=src, dst_ref=dst, send_sem=s, recv_sem=r,
            device_id=device, device_id_type=MESH,
        )
        copy.start()
        sent.append(copy)

    def arrived(dst, r):
        pltpu.make_async_remote_copy(
            src_ref=dst, dst_ref=dst, send_sem=r, recv_sem=r,
            device_id=mirror, device_id_type=MESH,
        ).wait_recv()

    def groups(p):
        return (2 * p, 1, 2 - 2 * p)

    def slots(group):
        return pl.ds(PER * group, PER)

    mine = groups(parity)
    theirs = groups(1 - parity)

    P_FLOW, Q_FLOW, D_FLOW, F_FLOW = range(4)
    buffers = {P_FLOW: {1: p1, 2: p2}, Q_FLOW: {1: q1, 0: q0},
               D_FLOW: {0: d0, 1: d1}, F_FLOW: {1: f1, 0: f0}}
    order = {P_FLOW: (1, 2), Q_FLOW: (1, 0), D_FLOW: (0, 1), F_FLOW: (1, 0)}
    c_table = (c_p, c_q, c_d, c_f)
    t_table = (t_p, t_q, t_d, t_f)

    def piece(flow, half, g, row):
        return buffers[flow][g].at[half, row, pl.ds(0, PER)]

    def place(flow, g, row):
        return 2 * order[flow].index(g) + row

    def send_flows(*flows):
        for flow, device in flows:
            send(cols, c_table[flow].at[0], table_send.at[flow], table_recv.at[flow], device)
        for step in range(2):
            for row in range(ROWS):
                for flow, device in flows:
                    g = order[flow][step]
                    n = place(flow, g, row)
                    send(den.at[row, slots(mine[g])], piece(flow, 0, g, row),
                         send_s.at[flow, n], recv_s.at[flow, n], device)

    send_flows((Q_FLOW, q_chip), (P_FLOW, p_chip))
    send(cols, c_own, own_s.at[ROWS], own_r.at[ROWS], mirror)
    for row in range(ROWS):
        send(den.at[row], own1.at[row, pl.ds(0, NZ)], own_s.at[row], own_r.at[row], mirror)

    @pl.when(even_z)
    def _():
        pl.semaphore_wait(barrier, 2)

    send_flows((D_FLOW, d_to))

    def load_table(k, src, dst):
        copy = pltpu.make_async_copy(src, dst, table_s.at[k])
        copy.start()
        tables.append(copy)

    def flow_arrived(flow, step, row):
        g = order[flow][step]
        n = place(flow, g, row)
        arrived(piece(flow, 0, g, row), recv_s.at[flow, n])
        if flow == Q_FLOW:
            m = place(F_FLOW, g, row)
            send(piece(flow, 0, g, row), piece(F_FLOW, 0, g, row),
                 send_s.at[F_FLOW, m], recv_s.at[F_FLOW, m], f_to)
        send(piece(flow, 0, g, row), piece(flow, 1, g, row),
             mirror_s.at[flow, n], mirrored_s.at[flow, n], mirror)

    def mirrored(flow, g):
        for row in range(ROWS):
            arrived(piece(flow, 1, g, row), mirrored_s.at[flow, place(flow, g, row)])

    def table_arrived(flow):
        arrived(c_table[flow].at[0], table_recv.at[flow])
        if flow == Q_FLOW:
            send(c_q.at[0], c_f.at[0], table_send.at[F_FLOW], table_recv.at[F_FLOW], f_to)
        send(c_table[flow].at[0], c_table[flow].at[1], table_out.at[flow],
             table_back.at[flow], mirror)

    def first_of(device):
        return device[0] * (4 * ROWS) + device[1] * ROWS

    first, p_first, q_first = first_of((blk, inner)), first_of(p_chip), first_of(q_chip)

    def parts(lhs, rhs):
        product = jnp.dot(lhs, rhs, preferred_element_type=jnp.float32)
        width = den.shape[3]
        return [product[:, b * width:(b + 1) * width] for b in range(PER)]

    def entries(table, index, group):
        return [table[(*index, PER * group + b)] for b in range(PER)]

    def add(i, group, blocks, fresh=False):
        for b, block in enumerate(blocks):
            if fresh:
                out[i, PER * group + b] = 2.0 * own0[i, PER * group + b] - block
            else:
                out[i, PER * group + b] -= block

    pair = [(half, row) for half in range(2) for row in range(ROWS)]

    def products(target, left, wanted):
        names, reads = left
        lhs = left_side([read(find(name, target, range(PER), 0))
                         for name, read in zip(names, reads)])
        present = [find(name, target, (1, 1, 1), 0) == 1 for name in names]
        for (columns, blocks), want in wanted:
            columns = [[jnp.where(there, c, -1) for c in row]
                       for there, row in zip(present, columns)]
            rhs = right_side([
                [read(find(row, column, range(PER), empty))
                 for row, (read, empty) in zip(columns, blocks)]
                for column in want
            ])
            yield parts(lhs, rhs)

    def of_flow(flow, g, parity_there):
        buffer = buffers[flow][g]
        names = [entries(t_table[flow], index, groups(parity_there)[g]) for index in pair]
        reads = [lambda s, index=index: buffer[(*index, s)] for index in pair]
        return names, reads

    def right_of_flow(flow, g, parity_there):
        names, reads = of_flow(flow, g, parity_there)
        return names, [(read, PER) for read in reads]

    def of_own(group):
        names = [entries(t_own, index, group) for index in pair]
        reads = [lambda s, buffer=(own0, own1)[half], row=row: buffer[row, PER * group + s]
                 for half, row in pair]
        return names, reads

    def right_of_own(group):
        names, reads = of_own(group)
        return names, [(read, NZ - PER * group) for read in reads]

    def want(i, group):
        return entries(t_own, (0, i), group)

    def own_products(i):
        for e, blocks in enumerate(products(
                first + i, of_own(1), [(right_of_own(e), want(i, e)) for e in range(3)])):
            add(i, e, blocks, fresh=True)

    def store(ref, k, i, blocks, fresh=False):
        for b, block in enumerate(blocks):
            if fresh:
                ref[k, i, b] = block
            else:
                ref[k, i, b] += block

    def q_own(i):
        wanted = [(right_of_own(mine[2]), entries(t_q, (0, i), 1)),
                  (right_of_own(1), entries(t_q, (0, i), theirs[2]))]
        for k, blocks in enumerate(products(q_first + i, of_own(mine[2]), wanted)):
            store(q_out, k, i, blocks, fresh=True)

    def q_part(k, i):
        g = (1, 2)[k]
        (blocks,) = products(q_first + i, of_flow(P_FLOW, 1, 1 - parity), [
            (right_of_flow(P_FLOW, g, 1 - parity), entries(t_q, (0, i), theirs[g]))])
        store(q_out, k, i, blocks)

    def p_part(k, i):
        g = (0, 1)[k]
        (blocks,) = products(p_first + i, of_flow(D_FLOW, 0, parity), [
            (right_of_flow(D_FLOW, g, parity), entries(t_p, (0, i), theirs[(1, 0)[k]]))])
        store(p_out, k, i, blocks, fresh=k == 0)

    def p_part_q(i):
        (blocks,) = products(p_first + i, of_flow(Q_FLOW, 1, 1 - parity), [
            (right_of_flow(Q_FLOW, 0, 1 - parity), entries(t_p, (0, i), theirs[0]))])
        store(p_out, 1, i, blocks, fresh=True)

    def from_p(i):
        wanted = [(right_of_flow(P_FLOW, 2, 1 - parity), want(i, 1)),
                  (right_of_flow(P_FLOW, 1, 1 - parity), want(i, mine[2]))]
        for group, blocks in zip((1, mine[2]), products(
                first + i, of_flow(P_FLOW, 2, 1 - parity), wanted)):
            add(i, group, blocks)

    def from_f(i):
        wanted = [(right_of_flow(F_FLOW, 0, 1 - parity), want(i, 1)),
                  (right_of_flow(F_FLOW, 1, 1 - parity), want(i, mine[0]))]
        for group, blocks in zip((1, mine[0]), products(
                first + i, of_flow(F_FLOW, 0, 1 - parity), wanted)):
            add(i, group, blocks)

    def each_row(*steps):
        def body(i, carry):
            for step in steps:
                step(i)
            return carry
        lax.fori_loop(0, ROWS, body, 0)

    def send_part(n, k, i):
        src, dst, device = ((q_out, q_in, q_chip), (p_out, p_in, p_chip))[n]
        send(src.at[k, i], dst.at[k, i], part_s.at[n, 2 * k + i], part_r.at[n, 2 * k + i],
             device)

    def part_arrived(k, i):
        for n, (ref, group) in enumerate(((q_in, (1, mine[2])[k]), (p_in, (1, mine[0])[k]))):
            arrived(ref.at[k, i], part_r.at[n, 2 * k + i])
            add(i, group, [ref[k, i, b] for b in range(PER)])

    def tables_ready(*flows):
        for flow in flows:
            arrived(c_table[flow].at[1], table_back.at[flow])
            load_table(2 + flow, c_table[flow], t_table[flow])
        for copy in tables[-len(flows):]:
            copy.wait()

    table_arrived(Q_FLOW)
    table_arrived(P_FLOW)
    arrived(c_own, own_r.at[ROWS])
    load_table(1, c_own, t_own.at[1])
    for copy in owned:
        copy.wait()
    for row in range(ROWS):
        arrived(own1.at[row, pl.ds(0, NZ)], own_r.at[row])
    for k in range(2):
        tables[k].wait()
    each_row(own_products)
    flow_arrived(Q_FLOW, 0, 0)
    flow_arrived(P_FLOW, 0, 0)
    tables_ready(P_FLOW, Q_FLOW)
    each_row(q_own)
    flow_arrived(Q_FLOW, 0, 1)
    flow_arrived(P_FLOW, 0, 1)
    mirrored(P_FLOW, 1)
    each_row(lambda i: q_part(0, i))
    table_arrived(D_FLOW)
    table_arrived(F_FLOW)
    flow_arrived(D_FLOW, 0, 0)
    flow_arrived(D_FLOW, 0, 1)
    for i in range(ROWS):
        send_part(0, 0, i)
    flow_arrived(Q_FLOW, 1, 0)
    flow_arrived(P_FLOW, 1, 0)
    tables_ready(D_FLOW, F_FLOW)
    mirrored(D_FLOW, 0)
    each_row(lambda i: p_part(0, i))
    flow_arrived(F_FLOW, 0, 0)
    for i in range(ROWS):
        send_part(1, 0, i)
    flow_arrived(Q_FLOW, 1, 1)
    flow_arrived(P_FLOW, 1, 1)
    mirrored(Q_FLOW, 1)
    mirrored(P_FLOW, 2)
    flow_arrived(D_FLOW, 1, 0)
    for i in range(ROWS):
        q_part(1, i)
        send_part(0, 1, i)
    flow_arrived(D_FLOW, 1, 1)
    mirrored(Q_FLOW, 0)
    each_row(p_part_q)
    mirrored(D_FLOW, 1)
    for i in range(ROWS):
        p_part(1, i)
        send_part(1, 1, i)
    flow_arrived(F_FLOW, 0, 1)
    flow_arrived(F_FLOW, 1, 0)
    flow_arrived(F_FLOW, 1, 1)
    each_row(from_p)
    mirrored(F_FLOW, 1)
    mirrored(F_FLOW, 0)
    each_row(from_f)
    for k in range(2):
        for i in range(ROWS):
            part_arrived(k, i)
    for copy in sent:
        copy.wait_send()


def purified_rows(density, block_cols):
    rows, nz, b, _ = density.shape
    f32, i32 = density.dtype, jnp.int32
    dma = pltpu.SemaphoreType.DMA
    anywhere = pl.BlockSpec(memory_space=pl.ANY)
    vmem, smem = pltpu.VMEM, pltpu.SMEM
    return pl.pallas_call(
        purify_kernel,
        out_shape=jax.ShapeDtypeStruct(density.shape, f32),
        in_specs=[anywhere, anywhere],
        out_specs=pl.BlockSpec(memory_space=pltpu.VMEM),
        scratch_shapes=[
            *[vmem((rows, nz + 1, b, b), f32)] * 2,
            *[vmem((2, rows, PER + 1, b, b), f32)] * 8,
            *[vmem((2, rows, PER, b, b), f32)] * 4,
            vmem((rows, nz), i32), *[vmem((2, rows, nz), i32)] * 4,
            *[smem((2, rows, nz), i32)] * 5,
            dma((4, 4)), dma((4, 4)), dma((4, 4)), dma((4, 4)),
            dma((3,)), dma((3,)), dma((4,)), dma((4,)), dma((4,)), dma((4,)),
            dma((2, 4)), dma((2, 4)), dma((2,)), dma((6,)),
        ],
        compiler_params=pltpu.CompilerParams(
            collective_id=0, has_side_effects=True, vmem_limit_bytes=24 * 2**20),
    )(pltpu.with_memory_space_constraint(density, pltpu.HBM),
      pltpu.with_memory_space_constraint(block_cols, pltpu.HBM))


def shards(density, block_cols, targets):
    del targets
    return purified_rows(density, block_cols)


def solution(mesh):
    return jax.shard_map(
        shards,
        mesh=mesh,
        in_specs=(
            P(("blk", "inner"), None, None, None),
            P(("blk", "inner"), None),
            P(("blk", "inner"), None, None),
        ),
        out_specs=P(("blk", "inner"), None, None, None),
        check_vma=False,
    )
```

```python
import jax
import jax.numpy as jnp
from jax import lax
from jax.experimental import pallas as pl
from jax.experimental.pallas import tpu as pltpu
from jax.sharding import PartitionSpec as P

MESH = pl.DeviceIdType.MESH
PER = 3
NZ = 9
X = 4
Z = 8
Z = 8
ROWS = 2


def split(value):
    high = value.astype(jnp.bfloat16)
    return high, (value - high.astype(jnp.float32)).astype(jnp.bfloat16)


def find(columns, wanted, places, otherwise):
    place = jnp.int32(otherwise)
    for column, here in zip(columns, places):
        place = jnp.where(column == wanted, here, place)
    return place


def left_side(blocks):
    highs, lows = zip(*(split(block.T) for block in blocks))
    return jnp.concatenate(highs + lows + highs, axis=1)


def right_side(columns_of_blocks):
    columns = []
    for blocks in columns_of_blocks:
        highs, lows = zip(*(split(block) for block in blocks))
        columns.append(jnp.concatenate(highs + highs + lows, axis=0))
    return jnp.concatenate(columns, axis=1)


def purify_kernel(
    den, cols, out,
    own0, own1, p1, p2, q0, q1, d0, d1, f0, f1, p_out, p_in, q_out, q_in,
    c_own, c_p, c_q, c_d, c_f, t_own, t_p, t_q, t_d, t_f,
    send_s, recv_s, mirror_s, mirrored_s, own_s, own_r, table_send, table_recv,
    table_out, table_back, part_s, part_r, local_s, table_s,
):
    blk = lax.axis_index("blk")
    inner = lax.axis_index("inner")
    strips = lax.axis_size("blk")
    parity = lax.rem(blk, 2)
    core = lax.rem(inner, 2)
    chip_x = 2 * (inner // 2) + parity

    def at_x(x):
        x = lax.rem(x, X)
        return (blk - parity + lax.rem(x, 2), 2 * (x // 2) + core)

    p_chip = at_x(chip_x + 1 + 2 * parity)
    q_chip = at_x(chip_x + 3 - 2 * parity)
    mirror = (blk, inner + 1 - 2 * core)
    f_to = (lax.rem(blk + strips + 2 - 4 * parity, strips), inner)
    d_to = (lax.rem(blk + strips - 2 + 4 * parity, strips), inner)

    barrier = pltpu.get_barrier_semaphore()
    for device in (p_chip, q_chip, mirror):
        pl.semaphore_signal(barrier, inc=1, device_id=device, device_id_type=MESH)

    owned = []
    for row in range(ROWS):
        copy = pltpu.make_async_copy(den.at[row], own0.at[row, pl.ds(0, NZ)], local_s.at[row])
        copy.start()
        owned.append(copy)
    tables = [pltpu.make_async_copy(cols, t_own.at[0], table_s.at[0])]
    tables[0].start()

    none = jnp.zeros(den.shape[2:], jnp.float32)
    for row in range(ROWS):
        own0[row, NZ] = none
        own1[row, NZ] = none
        for half in range(2):
            for buffer in (p1, p2, q0, q1, d0, d1, f0, f1):
                buffer[half, row, PER] = none

    plane = lax.rem(blk // 2, Z)
    early = (plane == 0) | (plane == 3) | (plane == 5)
    middle = (plane == 1) | (plane == 7)
    late = jnp.logical_not(early | middle)
    for when, before in ((early, 0), (middle, 1), (late, 2)):
        @pl.when(when)
        def _(count=3 + before):
            pl.semaphore_wait(barrier, count)

    for device in (f_to, d_to):
        pl.semaphore_signal(barrier, inc=1, device_id=device, device_id_type=MESH)

    sent = []

    def send(src, dst, s, r, device, start=True, record=True):
        copy = pltpu.make_async_remote_copy(
            src_ref=src, dst_ref=dst, send_sem=s, recv_sem=r,
            device_id=device, device_id_type=MESH,
        )
        if start:
            copy.start()
        if record:
            sent.append(copy)

    def arrived(dst, r):
        pltpu.make_async_remote_copy(
            src_ref=dst, dst_ref=dst, send_sem=r, recv_sem=r,
            device_id=mirror, device_id_type=MESH,
        ).wait_recv()

    def groups(p):
        return (2 * p, 1, 2 - 2 * p)

    def slots(group):
        return pl.ds(PER * group, PER)

    mine = groups(parity)
    theirs = groups(1 - parity)

    P_FLOW, Q_FLOW, D_FLOW, F_FLOW = range(4)
    buffers = {P_FLOW: {1: p1, 2: p2}, Q_FLOW: {1: q1, 0: q0},
               D_FLOW: {0: d0, 1: d1}, F_FLOW: {1: f1, 0: f0}}
    order = {P_FLOW: (1, 2), Q_FLOW: (1, 0), D_FLOW: (0, 1), F_FLOW: (1, 0)}
    c_table = (c_p, c_q, c_d, c_f)
    t_table = (t_p, t_q, t_d, t_f)

    def piece(flow, half, g, row):
        return buffers[flow][g].at[half, row, pl.ds(0, PER)]

    def place(flow, g, row):
        return 2 * order[flow].index(g) + row

    def send_flows(*flows, **what):
        for flow, device in flows:
            send(cols, c_table[flow].at[0], table_send.at[flow], table_recv.at[flow], device, **what)
        for step in range(2):
            for row in range(ROWS):
                for flow, device in flows:
                    g = order[flow][step]
                    n = place(flow, g, row)
                    send(den.at[row, slots(mine[g])], piece(flow, 0, g, row),
                         send_s.at[flow, n], recv_s.at[flow, n], device, **what)

    send_flows((Q_FLOW, q_chip), (P_FLOW, p_chip))
    send(cols, c_own, own_s.at[ROWS], own_r.at[ROWS], mirror)
    for row in range(ROWS):
        send(den.at[row], own1.at[row, pl.ds(0, NZ)], own_s.at[row], own_r.at[row], mirror)

    known = late | (middle & ((plane == 1) == (parity == 0)))

    @pl.when(known)
    def _():
        send_flows((D_FLOW, d_to), record=False)

    for when, after in ((early, 2), (middle, 1)):
        @pl.when(when)
        def _(count=after):
            pl.semaphore_wait(barrier, count)

    @pl.when(jnp.logical_not(known))
    def _():
        send_flows((D_FLOW, d_to), record=False)

    send_flows((D_FLOW, d_to), start=False)

    def load_table(k, src, dst):
        copy = pltpu.make_async_copy(src, dst, table_s.at[k])
        copy.start()
        tables.append(copy)

    def flow_arrived(flow, step, row):
        g = order[flow][step]
        n = place(flow, g, row)
        arrived(piece(flow, 0, g, row), recv_s.at[flow, n])
        if flow == Q_FLOW:
            m = place(F_FLOW, g, row)
            send(piece(flow, 0, g, row), piece(F_FLOW, 0, g, row),
                 send_s.at[F_FLOW, m], recv_s.at[F_FLOW, m], f_to)
        send(piece(flow, 0, g, row), piece(flow, 1, g, row),
             mirror_s.at[flow, n], mirrored_s.at[flow, n], mirror)

    def mirrored(flow, g):
        for row in range(ROWS):
            arrived(piece(flow, 1, g, row), mirrored_s.at[flow, place(flow, g, row)])

    def table_arrived(flow):
        arrived(c_table[flow].at[0], table_recv.at[flow])
        if flow == Q_FLOW:
            send(c_q.at[0], c_f.at[0], table_send.at[F_FLOW], table_recv.at[F_FLOW], f_to)
        send(c_table[flow].at[0], c_table[flow].at[1], table_out.at[flow],
             table_back.at[flow], mirror)

    def first_of(device):
        return device[0] * (4 * ROWS) + device[1] * ROWS

    first, p_first, q_first = first_of((blk, inner)), first_of(p_chip), first_of(q_chip)

    def parts(lhs, rhs):
        product = jnp.dot(lhs, rhs, preferred_element_type=jnp.float32)
        width = den.shape[3]
        return [product[:, b * width:(b + 1) * width] for b in range(PER)]

    def entries(table, index, group):
        return [table[(*index, PER * group + b)] for b in range(PER)]

    def add(i, group, blocks, fresh=False):
        for b, block in enumerate(blocks):
            if fresh:
                out[i, PER * group + b] = 2.0 * own0[i, PER * group + b] - block
            else:
                out[i, PER * group + b] -= block

    pair = [(half, row) for half in range(2) for row in range(ROWS)]

    def products(target, left, wanted):
        names, reads = left
        lhs = left_side([read(find(name, target, range(PER), 0))
                         for name, read in zip(names, reads)])
        present = [find(name, target, (1, 1, 1), 0) == 1 for name in names]
        for (columns, blocks), want in wanted:
            columns = [[jnp.where(there, c, -1) for c in row]
                       for there, row in zip(present, columns)]
            rhs = right_side([
                [read(find(row, column, range(PER), empty))
                 for row, (read, empty) in zip(columns, blocks)]
                for column in want
            ])
            yield parts(lhs, rhs)

    def of_flow(flow, g, parity_there):
        buffer = buffers[flow][g]
        names = [entries(t_table[flow], index, groups(parity_there)[g]) for index in pair]
        reads = [lambda s, index=index: buffer[(*index, s)] for index in pair]
        return names, reads

    def right_of_flow(flow, g, parity_there):
        names, reads = of_flow(flow, g, parity_there)
        return names, [(read, PER) for read in reads]

    def of_own(group):
        names = [entries(t_own, index, group) for index in pair]
        reads = [lambda s, buffer=(own0, own1)[half], row=row: buffer[row, PER * group + s]
                 for half, row in pair]
        return names, reads

    def right_of_own(group):
        names, reads = of_own(group)
        return names, [(read, NZ - PER * group) for read in reads]

    def want(i, group):
        return entries(t_own, (0, i), group)

    def own_products(i):
        for e, blocks in enumerate(products(
                first + i, of_own(1), [(right_of_own(e), want(i, e)) for e in range(3)])):
            add(i, e, blocks, fresh=True)

    def store(ref, k, i, blocks, fresh=False):
        for b, block in enumerate(blocks):
            if fresh:
                ref[k, i, b] = block
            else:
                ref[k, i, b] += block

    def q_own(i):
        wanted = [(right_of_own(mine[2]), entries(t_q, (0, i), 1)),
                  (right_of_own(1), entries(t_q, (0, i), theirs[2]))]
        for k, blocks in enumerate(products(q_first + i, of_own(mine[2]), wanted)):
            store(q_out, k, i, blocks, fresh=True)

    def q_part(k, i):
        g = (1, 2)[k]
        (blocks,) = products(q_first + i, of_flow(P_FLOW, 1, 1 - parity), [
            (right_of_flow(P_FLOW, g, 1 - parity), entries(t_q, (0, i), theirs[g]))])
        store(q_out, k, i, blocks)

    def p_part(k, i):
        g = (0, 1)[k]
        (blocks,) = products(p_first + i, of_flow(D_FLOW, 0, parity), [
            (right_of_flow(D_FLOW, g, parity), entries(t_p, (0, i), theirs[(1, 0)[k]]))])
        store(p_out, k, i, blocks, fresh=k == 0)

    def p_part_q(i):
        (blocks,) = products(p_first + i, of_flow(Q_FLOW, 1, 1 - parity), [
            (right_of_flow(Q_FLOW, 0, 1 - parity), entries(t_p, (0, i), theirs[0]))])
        store(p_out, 1, i, blocks, fresh=True)

    def from_p(i):
        wanted = [(right_of_flow(P_FLOW, 2, 1 - parity), want(i, 1)),
                  (right_of_flow(P_FLOW, 1, 1 - parity), want(i, mine[2]))]
        for group, blocks in zip((1, mine[2]), products(
                first + i, of_flow(P_FLOW, 2, 1 - parity), wanted)):
            add(i, group, blocks)

    def from_f(i):
        wanted = [(right_of_flow(F_FLOW, 0, 1 - parity), want(i, 1)),
                  (right_of_flow(F_FLOW, 1, 1 - parity), want(i, mine[0]))]
        for group, blocks in zip((1, mine[0]), products(
                first + i, of_flow(F_FLOW, 0, 1 - parity), wanted)):
            add(i, group, blocks)

    def each_row(*steps):
        def body(i, carry):
            for step in steps:
                step(i)
            return carry
        lax.fori_loop(0, ROWS, body, 0)

    def send_part(n, k, i):
        src, dst, device = ((q_out, q_in, q_chip), (p_out, p_in, p_chip))[n]
        send(src.at[k, i], dst.at[k, i], part_s.at[n, 2 * k + i], part_r.at[n, 2 * k + i],
             device)

    def part_arrived(k, i):
        for n, (ref, group) in enumerate(((q_in, (1, mine[2])[k]), (p_in, (1, mine[0])[k]))):
            arrived(ref.at[k, i], part_r.at[n, 2 * k + i])
            add(i, group, [ref[k, i, b] for b in range(PER)])

    def tables_ready(*flows):
        for flow in flows:
            arrived(c_table[flow].at[1], table_back.at[flow])
            load_table(2 + flow, c_table[flow], t_table[flow])
        for copy in tables[-len(flows):]:
            copy.wait()

    table_arrived(Q_FLOW)
    table_arrived(P_FLOW)
    arrived(c_own, own_r.at[ROWS])
    load_table(1, c_own, t_own.at[1])
    for copy in owned:
        copy.wait()
    for row in range(ROWS):
        arrived(own1.at[row, pl.ds(0, NZ)], own_r.at[row])
    for k in range(2):
        tables[k].wait()
    each_row(own_products)
    flow_arrived(Q_FLOW, 0, 0)
    flow_arrived(P_FLOW, 0, 0)
    tables_ready(P_FLOW, Q_FLOW)
    each_row(q_own)
    flow_arrived(Q_FLOW, 0, 1)
    flow_arrived(P_FLOW, 0, 1)
    mirrored(P_FLOW, 1)
    each_row(lambda i: q_part(0, i))
    table_arrived(D_FLOW)
    table_arrived(F_FLOW)
    flow_arrived(D_FLOW, 0, 0)
    flow_arrived(D_FLOW, 0, 1)
    for i in range(ROWS):
        send_part(0, 0, i)
    flow_arrived(Q_FLOW, 1, 0)
    flow_arrived(P_FLOW, 1, 0)
    tables_ready(D_FLOW, F_FLOW)
    mirrored(D_FLOW, 0)
    each_row(lambda i: p_part(0, i))
    flow_arrived(F_FLOW, 0, 0)
    for i in range(ROWS):
        send_part(1, 0, i)
    flow_arrived(Q_FLOW, 1, 1)
    flow_arrived(P_FLOW, 1, 1)
    mirrored(Q_FLOW, 1)
    mirrored(P_FLOW, 2)
    flow_arrived(D_FLOW, 1, 0)
    for i in range(ROWS):
        q_part(1, i)
        send_part(0, 1, i)
    flow_arrived(D_FLOW, 1, 1)
    mirrored(Q_FLOW, 0)
    each_row(p_part_q)
    mirrored(D_FLOW, 1)
    for i in range(ROWS):
        p_part(1, i)
        send_part(1, 1, i)
    flow_arrived(F_FLOW, 0, 1)
    flow_arrived(F_FLOW, 1, 0)
    flow_arrived(F_FLOW, 1, 1)
    each_row(from_p)
    mirrored(F_FLOW, 1)
    mirrored(F_FLOW, 0)
    each_row(from_f)
    for k in range(2):
        for i in range(ROWS):
            part_arrived(k, i)
    for copy in sent:
        copy.wait_send()


def purified_rows(density, block_cols):
    rows, nz, b, _ = density.shape
    f32, i32 = density.dtype, jnp.int32
    dma = pltpu.SemaphoreType.DMA
    anywhere = pl.BlockSpec(memory_space=pl.ANY)
    vmem, smem = pltpu.VMEM, pltpu.SMEM
    return pl.pallas_call(
        purify_kernel,
        out_shape=jax.ShapeDtypeStruct(density.shape, f32),
        in_specs=[anywhere, anywhere],
        out_specs=pl.BlockSpec(memory_space=pltpu.VMEM),
        scratch_shapes=[
            *[vmem((rows, nz + 1, b, b), f32)] * 2,
            *[vmem((2, rows, PER + 1, b, b), f32)] * 8,
            *[vmem((2, rows, PER, b, b), f32)] * 4,
            vmem((rows, nz), i32), *[vmem((2, rows, nz), i32)] * 4,
            *[smem((2, rows, nz), i32)] * 5,
            dma((4, 4)), dma((4, 4)), dma((4, 4)), dma((4, 4)),
            dma((3,)), dma((3,)), dma((4,)), dma((4,)), dma((4,)), dma((4,)),
            dma((2, 4)), dma((2, 4)), dma((2,)), dma((6,)),
        ],
        compiler_params=pltpu.CompilerParams(
            collective_id=0, has_side_effects=True, vmem_limit_bytes=24 * 2**20),
    )(pltpu.with_memory_space_constraint(density, pltpu.HBM),
      pltpu.with_memory_space_constraint(block_cols, pltpu.HBM))


def shards(density, block_cols, targets):
    del targets
    return purified_rows(density, block_cols)


def solution(mesh):
    return jax.shard_map(
        shards,
        mesh=mesh,
        in_specs=(
            P(("blk", "inner"), None, None, None),
            P(("blk", "inner"), None),
            P(("blk", "inner"), None, None),
        ),
        out_specs=P(("blk", "inner"), None, None, None),
        check_vma=False,
    )
```

```python
import jax
import jax.numpy as jnp
from jax import lax
from jax.experimental import pallas as pl
from jax.experimental.pallas import tpu as pltpu
from jax.sharding import PartitionSpec as P

MESH = pl.DeviceIdType.MESH
PER = 3
NZ = 9
X = 4
Z = 8
Z = 8
ROWS = 2


def split(value):
    high = value.astype(jnp.bfloat16)
    return high, (value - high.astype(jnp.float32)).astype(jnp.bfloat16)


def find(columns, wanted, places, otherwise):
    place = jnp.int32(otherwise)
    for column, here in zip(columns, places):
        place = jnp.where(column == wanted, here, place)
    return place


def left_side(blocks):
    highs, lows = zip(*(split(block.T) for block in blocks))
    return jnp.concatenate(highs + lows + highs, axis=1)


def right_side(columns_of_blocks):
    columns = []
    for blocks in columns_of_blocks:
        highs, lows = zip(*(split(block) for block in blocks))
        columns.append(jnp.concatenate(highs + highs + lows, axis=0))
    return jnp.concatenate(columns, axis=1)


def purify_kernel(
    den, cols, out,
    own0, own1, p1, p2, q0, q1, d0, d1, d1_far, f0, f1, p_out, p_in, q_out, q_in,
    c_own, c_p, c_q, c_d, c_f, t_own, t_p, t_q, t_d, t_f,
    send_s, recv_s, mirror_s, mirrored_s, own_s, own_r, table_send, table_recv,
    table_out, table_back, part_s, part_r, local_s, table_s,
):
    blk = lax.axis_index("blk")
    inner = lax.axis_index("inner")
    strips = lax.axis_size("blk")
    parity = lax.rem(blk, 2)
    core = lax.rem(inner, 2)
    chip_x = 2 * (inner // 2) + parity

    def at_x(x):
        x = lax.rem(x, X)
        return (blk - parity + lax.rem(x, 2), 2 * (x // 2) + core)

    p_chip = at_x(chip_x + 1 + 2 * parity)
    q_chip = at_x(chip_x + 3 - 2 * parity)
    mirror = (blk, inner + 1 - 2 * core)
    f_to = (lax.rem(blk + strips + 2 - 4 * parity, strips), inner)
    d_to = (lax.rem(blk + strips - 2 + 4 * parity, strips), inner)

    barrier = pltpu.get_barrier_semaphore()
    for device in (p_chip, q_chip, mirror):
        pl.semaphore_signal(barrier, inc=1, device_id=device, device_id_type=MESH)

    owned = []
    for row in range(ROWS):
        copy = pltpu.make_async_copy(den.at[row], own0.at[row, pl.ds(0, NZ)], local_s.at[row])
        copy.start()
        owned.append(copy)
    tables = [pltpu.make_async_copy(cols, t_own.at[0], table_s.at[0])]
    tables[0].start()

    none = jnp.zeros(den.shape[2:], jnp.float32)
    for row in range(ROWS):
        own0[row, NZ] = none
        own1[row, NZ] = none
        for half in range(2):
            for buffer in (p1, p2, q0, q1, d0, f0, f1):
                buffer[half, row, PER] = none
            (d1, d1_far)[half][row, PER] = none

    plane = lax.rem(blk // 2, Z)
    early = (plane == 0) | (plane == 3) | (plane == 5)
    middle = (plane == 1) | (plane == 7)
    late = jnp.logical_not(early | middle)
    for when, before in ((early, 0), (middle, 1), (late, 2)):
        @pl.when(when)
        def _(count=3 + before):
            pl.semaphore_wait(barrier, count)

    for device in (f_to, d_to):
        pl.semaphore_signal(barrier, inc=1, device_id=device, device_id_type=MESH)

    sent = []

    def send(src, dst, s, r, device, start=True, record=True):
        copy = pltpu.make_async_remote_copy(
            src_ref=src, dst_ref=dst, send_sem=s, recv_sem=r,
            device_id=device, device_id_type=MESH,
        )
        if start:
            copy.start()
        if record:
            sent.append(copy)

    def arrived(dst, r):
        pltpu.make_async_remote_copy(
            src_ref=dst, dst_ref=dst, send_sem=r, recv_sem=r,
            device_id=mirror, device_id_type=MESH,
        ).wait_recv()

    def groups(p):
        return (2 * p, 1, 2 - 2 * p)

    def slots(group):
        return pl.ds(PER * group, PER)

    mine = groups(parity)
    theirs = groups(1 - parity)

    P_FLOW, Q_FLOW, D_FLOW, F_FLOW = range(4)
    buffers = {P_FLOW: {1: p1, 2: p2}, Q_FLOW: {1: q1, 0: q0},
               D_FLOW: {0: d0, 1: (d1, d1_far)}, F_FLOW: {1: f1, 0: f0}}
    order = {P_FLOW: (1, 2), Q_FLOW: (1, 0), D_FLOW: (0, 1), F_FLOW: (1, 0)}
    c_table = (c_p, c_q, c_d, c_f)
    t_table = (t_p, t_q, t_d, t_f)

    def piece(flow, half, g, row):
        buffer = buffers[flow][g]
        if isinstance(buffer, tuple):
            return buffer[half].at[row, pl.ds(0, PER)]
        return buffer.at[half, row, pl.ds(0, PER)]

    def place(flow, g, row):
        return 2 * order[flow].index(g) + row

    def send_flows(*flows, **what):
        for flow, device in flows:
            send(cols, c_table[flow].at[0], table_send.at[flow], table_recv.at[flow], device, **what)
        for step in range(2):
            for row in range(ROWS):
                for flow, device in flows:
                    g = order[flow][step]
                    n = place(flow, g, row)
                    send(den.at[row, slots(mine[g])], piece(flow, 0, g, row),
                         send_s.at[flow, n], recv_s.at[flow, n], device, **what)

    send_flows((Q_FLOW, q_chip), (P_FLOW, p_chip))
    send(cols, c_own, own_s.at[ROWS], own_r.at[ROWS], mirror)
    for row in range(ROWS):
        send(den.at[row], own1.at[row, pl.ds(0, NZ)], own_s.at[row], own_r.at[row], mirror)

    known = late | (middle & ((plane == 1) == (parity == 0)))

    @pl.when(known)
    def _():
        send_flows((D_FLOW, d_to), record=False)

    for when, after in ((early, 2), (middle, 1)):
        @pl.when(when)
        def _(count=after):
            pl.semaphore_wait(barrier, count)

    @pl.when(jnp.logical_not(known))
    def _():
        send_flows((D_FLOW, d_to), record=False)

    send_flows((D_FLOW, d_to), start=False)

    def load_table(k, src, dst):
        copy = pltpu.make_async_copy(src, dst, table_s.at[k])
        copy.start()
        tables.append(copy)

    def flow_arrived(flow, step, row):
        g = order[flow][step]
        n = place(flow, g, row)
        arrived(piece(flow, 0, g, row), recv_s.at[flow, n])
        if flow == Q_FLOW:
            m = place(F_FLOW, g, row)
            send(piece(flow, 0, g, row), piece(F_FLOW, 0, g, row),
                 send_s.at[F_FLOW, m], recv_s.at[F_FLOW, m], f_to)
        send(piece(flow, 0, g, row), piece(flow, 1, g, row),
             mirror_s.at[flow, n], mirrored_s.at[flow, n], mirror)

    def mirrored(flow, g):
        for row in range(ROWS):
            arrived(piece(flow, 1, g, row), mirrored_s.at[flow, place(flow, g, row)])

    def table_arrived(flow):
        arrived(c_table[flow].at[0], table_recv.at[flow])
        if flow == Q_FLOW:
            send(c_q.at[0], c_f.at[0], table_send.at[F_FLOW], table_recv.at[F_FLOW], f_to)
        send(c_table[flow].at[0], c_table[flow].at[1], table_out.at[flow],
             table_back.at[flow], mirror)

    def first_of(device):
        return device[0] * (4 * ROWS) + device[1] * ROWS

    first, p_first, q_first = first_of((blk, inner)), first_of(p_chip), first_of(q_chip)

    def parts(lhs, rhs):
        product = jnp.dot(lhs, rhs, preferred_element_type=jnp.float32)
        width = den.shape[3]
        return [product[:, b * width:(b + 1) * width] for b in range(PER)]

    def entries(table, index, group):
        return [table[(*index, PER * group + b)] for b in range(PER)]

    def add(i, group, blocks, fresh=False):
        for b, block in enumerate(blocks):
            if fresh:
                out[i, PER * group + b] = 2.0 * own0[i, PER * group + b] - block
            else:
                out[i, PER * group + b] -= block

    pair = [(half, row) for half in range(2) for row in range(ROWS)]

    def products(target, left, wanted):
        names, reads = left
        lhs = left_side([read(find(name, target, range(PER), 0))
                         for name, read in zip(names, reads)])
        present = [find(name, target, (1, 1, 1), 0) == 1 for name in names]
        for (columns, blocks), want in wanted:
            columns = [[jnp.where(there, c, -1) for c in row]
                       for there, row in zip(present, columns)]
            rhs = right_side([
                [read(find(row, column, range(PER), empty))
                 for row, (read, empty) in zip(columns, blocks)]
                for column in want
            ])
            yield parts(lhs, rhs)

    def of_flow(flow, g, parity_there, where=pair):
        buffer = buffers[flow][g]
        names = [entries(t_table[flow], index, groups(parity_there)[g]) for index in where]
        if isinstance(buffer, tuple):
            reads = [lambda s, half=half, row=row: buffer[half][row, s] for half, row in where]
        else:
            reads = [lambda s, index=index: buffer[(*index, s)] for index in where]
        return names, reads

    def right_of_flow(flow, g, parity_there, where=pair):
        names, reads = of_flow(flow, g, parity_there, where)
        return names, [(read, PER) for read in reads]

    def of_own(group):
        names = [entries(t_own, index, group) for index in pair]
        reads = [lambda s, buffer=(own0, own1)[half], row=row: buffer[row, PER * group + s]
                 for half, row in pair]
        return names, reads

    def right_of_own(group):
        names, reads = of_own(group)
        return names, [(read, NZ - PER * group) for read in reads]

    def want(i, group):
        return entries(t_own, (0, i), group)

    def own_products(i):
        for e, blocks in enumerate(products(
                first + i, of_own(1), [(right_of_own(e), want(i, e)) for e in range(3)])):
            add(i, e, blocks, fresh=True)

    def store(ref, k, i, blocks, fresh=False):
        for b, block in enumerate(blocks):
            if fresh:
                ref[k, i, b] = block
            else:
                ref[k, i, b] += block

    def q_own(i):
        wanted = [(right_of_own(mine[2]), entries(t_q, (0, i), 1)),
                  (right_of_own(1), entries(t_q, (0, i), theirs[2]))]
        for k, blocks in enumerate(products(q_first + i, of_own(mine[2]), wanted)):
            store(q_out, k, i, blocks, fresh=True)

    def q_part(k, i):
        g = (1, 2)[k]
        (blocks,) = products(q_first + i, of_flow(P_FLOW, 1, 1 - parity), [
            (right_of_flow(P_FLOW, g, 1 - parity), entries(t_q, (0, i), theirs[g]))])
        store(q_out, k, i, blocks)

    def p_part(k, i, where=pair):
        g = (0, 1)[k]
        (blocks,) = products(p_first + i, of_flow(D_FLOW, 0, parity, where), [
            (right_of_flow(D_FLOW, g, parity, where), entries(t_p, (0, i), theirs[(1, 0)[k]]))])
        store(p_out, k, i, blocks, fresh=k == 0)

    def p_part_q(i):
        (blocks,) = products(p_first + i, of_flow(Q_FLOW, 1, 1 - parity), [
            (right_of_flow(Q_FLOW, 0, 1 - parity), entries(t_p, (0, i), theirs[0]))])
        store(p_out, 1, i, blocks, fresh=True)

    def from_p(i):
        wanted = [(right_of_flow(P_FLOW, 2, 1 - parity), want(i, 1)),
                  (right_of_flow(P_FLOW, 1, 1 - parity), want(i, mine[2]))]
        for group, blocks in zip((1, mine[2]), products(
                first + i, of_flow(P_FLOW, 2, 1 - parity), wanted)):
            add(i, group, blocks)

    def from_f(i):
        wanted = [(right_of_flow(F_FLOW, 0, 1 - parity), want(i, 1)),
                  (right_of_flow(F_FLOW, 1, 1 - parity), want(i, mine[0]))]
        for group, blocks in zip((1, mine[0]), products(
                first + i, of_flow(F_FLOW, 0, 1 - parity), wanted)):
            add(i, group, blocks)

    def each_row(*steps):
        def body(i, carry):
            for step in steps:
                step(i)
            return carry
        lax.fori_loop(0, ROWS, body, 0)

    def send_part(n, k, i):
        src, dst, device = ((q_out, q_in, q_chip), (p_out, p_in, p_chip))[n]
        send(src.at[k, i], dst.at[k, i], part_s.at[n, 2 * k + i], part_r.at[n, 2 * k + i],
             device)

    def part_arrived(k, i):
        for n, (ref, group) in enumerate(((q_in, (1, mine[2])[k]), (p_in, (1, mine[0])[k]))):
            arrived(ref.at[k, i], part_r.at[n, 2 * k + i])
            add(i, group, [ref[k, i, b] for b in range(PER)])

    def tables_ready(*flows):
        for flow in flows:
            arrived(c_table[flow].at[1], table_back.at[flow])
            load_table(2 + flow, c_table[flow], t_table[flow])
        for copy in tables[-len(flows):]:
            copy.wait()

    table_arrived(Q_FLOW)
    table_arrived(P_FLOW)
    arrived(c_own, own_r.at[ROWS])
    load_table(1, c_own, t_own.at[1])
    for copy in owned:
        copy.wait()
    for row in range(ROWS):
        arrived(own1.at[row, pl.ds(0, NZ)], own_r.at[row])
    for k in range(2):
        tables[k].wait()
    each_row(own_products)
    flow_arrived(Q_FLOW, 0, 0)
    flow_arrived(P_FLOW, 0, 0)
    tables_ready(P_FLOW, Q_FLOW)
    each_row(q_own)
    flow_arrived(Q_FLOW, 0, 1)
    flow_arrived(P_FLOW, 0, 1)
    mirrored(P_FLOW, 1)
    each_row(lambda i: q_part(0, i))
    table_arrived(D_FLOW)
    table_arrived(F_FLOW)
    flow_arrived(D_FLOW, 0, 0)
    flow_arrived(D_FLOW, 0, 1)
    for i in range(ROWS):
        send_part(0, 0, i)
    flow_arrived(Q_FLOW, 1, 0)
    flow_arrived(P_FLOW, 1, 0)
    tables_ready(D_FLOW, F_FLOW)
    mirrored(D_FLOW, 0)
    each_row(lambda i: p_part(0, i))
    flow_arrived(F_FLOW, 0, 0)
    for i in range(ROWS):
        send_part(1, 0, i)
    flow_arrived(Q_FLOW, 1, 1)
    flow_arrived(P_FLOW, 1, 1)
    mirrored(Q_FLOW, 1)
    mirrored(P_FLOW, 2)
    flow_arrived(D_FLOW, 1, 0)
    for i in range(ROWS):
        q_part(1, i)
        send_part(0, 1, i)
    flow_arrived(D_FLOW, 1, 1)
    mirrored(Q_FLOW, 0)
    each_row(p_part_q)
    near, far = pair[:ROWS], pair[ROWS:]
    each_row(lambda i: p_part(1, i, near))
    mirrored(D_FLOW, 1)
    for i in range(ROWS):
        p_part(1, i, far)
        send_part(1, 1, i)
    flow_arrived(F_FLOW, 0, 1)
    flow_arrived(F_FLOW, 1, 0)
    flow_arrived(F_FLOW, 1, 1)
    each_row(from_p)
    mirrored(F_FLOW, 1)
    mirrored(F_FLOW, 0)
    each_row(from_f)
    for k in range(2):
        for i in range(ROWS):
            part_arrived(k, i)
    for copy in sent:
        copy.wait_send()


def purified_rows(density, block_cols):
    rows, nz, b, _ = density.shape
    f32, i32 = density.dtype, jnp.int32
    dma = pltpu.SemaphoreType.DMA
    anywhere = pl.BlockSpec(memory_space=pl.ANY)
    vmem, smem = pltpu.VMEM, pltpu.SMEM
    return pl.pallas_call(
        purify_kernel,
        out_shape=jax.ShapeDtypeStruct(density.shape, f32),
        in_specs=[anywhere, anywhere],
        out_specs=pl.BlockSpec(memory_space=pltpu.VMEM),
        scratch_shapes=[
            *[vmem((rows, nz + 1, b, b), f32)] * 2,
            *[vmem((2, rows, PER + 1, b, b), f32)] * 5,
            *[vmem((rows, PER + 1, b, b), f32)] * 2,
            *[vmem((2, rows, PER + 1, b, b), f32)] * 2,
            *[vmem((2, rows, PER, b, b), f32)] * 4,
            vmem((rows, nz), i32), *[vmem((2, rows, nz), i32)] * 4,
            *[smem((2, rows, nz), i32)] * 5,
            dma((4, 4)), dma((4, 4)), dma((4, 4)), dma((4, 4)),
            dma((3,)), dma((3,)), dma((4,)), dma((4,)), dma((4,)), dma((4,)),
            dma((2, 4)), dma((2, 4)), dma((2,)), dma((6,)),
        ],
        compiler_params=pltpu.CompilerParams(
            collective_id=0, has_side_effects=True, vmem_limit_bytes=24 * 2**20),
    )(pltpu.with_memory_space_constraint(density, pltpu.HBM),
      pltpu.with_memory_space_constraint(block_cols, pltpu.HBM))


def shards(density, block_cols, targets):
    del targets
    return purified_rows(density, block_cols)


def solution(mesh):
    return jax.shard_map(
        shards,
        mesh=mesh,
        in_specs=(
            P(("blk", "inner"), None, None, None),
            P(("blk", "inner"), None),
            P(("blk", "inner"), None, None),
        ),
        out_specs=P(("blk", "inner"), None, None, None),
        check_vma=False,
    )
```
